256 devices in a mesh: leaf: 16 (over y, z_lo), draw: 16 (over z_hi, x, core).
Axes of the slice: x: 4, y: 4, z: 8 (z_hi: 2, z_lo: 4; z = z_hi * 4 + z_lo), core: 2. Of those that a mesh axis runs over, the one named last changes fastest.
Arguments:
- noise_draws: bfloat16 [3, 32, 256, 8192], P(None, 'leaf', None, 'draw'), may hold values from -6 to 6
- inverse_diagonal: bfloat16 [3, 32, 256, 256], P(None, 'leaf', 'draw'), as said below
- coupling_blocks: bfloat16 [2, 32, 16, 256, 256], P(None, 'leaf', 'draw'), may hold values from -0.0625 to 0.0625
- ancestor_pick: int32 [2, 16, 16], replicated, may hold values from 0 to 1
- coupling_lists: int32 [2, 32, 16], P(None, 'leaf'), may hold values from 0 to 31, as said below
- live_counts: int32 [2, 32], P(None, 'leaf'), may hold values from 1 to 16, as said below
Outputs:
- samples: bfloat16 [3, 32, 256, 8192], P(None, 'leaf', None, 'draw')
The draws below stay inside these ranges and needn't reach their ends.
Inputs may be any that keep to these rules, and one draw needn't show every extreme that they name: `coupling_lists`: the 16 entries of one supernode are distinct. Level 1 entries are below 16, and the live entries of the 2 level-1 supernodes of one owner together name every owner. In level 2 the first 8 entries are 16 or more and the rest below 16; the first halves of one owner's level-2 supernodes together name every value from 16 to 31. `live_counts`: the level-1 counts of one owner's 2 supernodes sum to more than 16; level-2 counts are 8 or more; in each level some supernode has 16. `inverse_diagonal`: each block is lower triangular, with diagonal entries between 0.6 and 1.4.
All inputs are finite; a program needn't handle non-finite values.
Results may differ from the reference program's by a relative error of at most 0.0052.
Values may be sent and summed in bfloat16 or wider, within the bound.
A program may use at most 64 MiB of HBM per device.

```python
import jax
import jax.numpy as jnp
from jax import lax

W = 256
NODES_DEV = 2
LEVELS = 3
OWNERS = 16
COUPLE = 16
NODES = 32
S = 8192


def owner_orders(seed_key, rows, owners):
    scores = jax.random.randint(seed_key, (rows, owners), 0, 1 << 20, dtype=jnp.int32)
    scores = scores * owners + lax.broadcasted_iota(jnp.int32, (rows, owners), 1)
    return jnp.argsort(scores, axis=1, stable=True).astype(jnp.int32)


def coupling_structure(base_key):
    owners = NODES // NODES_DEV
    half = COUPLE // 2
    keys = jax.random.split(jax.random.fold_in(base_key, 4099), 8)
    first_order = owner_orders(keys[0], owners, owners)
    level_one = jnp.stack([first_order, first_order[:, ::-1]], axis=1).reshape(NODES, COUPLE)
    upper_order = owner_orders(keys[1], owners, owners) + owners
    lower_order = owner_orders(keys[2], owners, owners)
    node_zero = jnp.concatenate([upper_order[:, :half], lower_order[:, :half]], axis=1)
    node_one = jnp.concatenate([upper_order[:, half:], lower_order[:, half:]], axis=1)
    level_two = jnp.stack([node_zero, node_one], axis=1).reshape(NODES, COUPLE)
    lists = jnp.stack([level_one, level_two], axis=0).astype(jnp.int32)
    first_count = jax.random.randint(keys[3], (owners,), 1, COUPLE + 1, dtype=jnp.int32)
    extra = jax.random.randint(keys[4], (owners,), 0, COUPLE, dtype=jnp.int32)
    second_count = COUPLE + 1 - first_count + extra % first_count
    count_one = jnp.stack([first_count, second_count], axis=1).reshape(NODES)
    count_two = jax.random.randint(keys[5], (NODES,), half, COUPLE + 1, dtype=jnp.int32)
    positions = lax.broadcasted_iota(jnp.int32, (NODES,), 0)
    chosen_one = jax.random.randint(keys[6], (), 0, NODES, dtype=jnp.int32)
    chosen_two = jax.random.randint(keys[7], (), 0, NODES, dtype=jnp.int32)
    count_one = jnp.where(positions == chosen_one, COUPLE, count_one)
    count_two = jnp.where(positions == chosen_two, COUPLE, count_two)
    counts = jnp.stack([count_one, count_two], axis=0).astype(jnp.int32)
    return (lists, counts)


def draw_coupling_lists(key, part):
    return coupling_structure(key)[0]


def draw_live_counts(key, part):
    return coupling_structure(key)[1]


def draw_inverse_diagonal(key, part):
    key_rough, key_diag = jax.random.split(jax.random.fold_in(key, 811))
    shape = (LEVELS, NODES, W, W)
    rough = jax.random.normal(key_rough, shape, jnp.float32)
    rows = lax.broadcasted_iota(jnp.int32, (W, W), 0)
    cols = lax.broadcasted_iota(jnp.int32, (W, W), 1)
    lower = (rows > cols).astype(jnp.float32)
    unit = (rows == cols).astype(jnp.float32)
    diagonal = jax.random.uniform(key_diag, (LEVELS, NODES, 1, W), jnp.float32, 0.6, 1.4)
    return (rough * lower * (0.8 / W ** 0.5) + unit * diagonal).astype(jnp.bfloat16)


def place_ends(array, rng, smallest, top_value):
    longest = array.shape.index(max(array.shape))
    spots = []
    for shift in (0, 1):
        where = [jax.random.randint(jax.random.fold_in(rng, axis), (), 0, length) for axis, length in enumerate(array.shape)]
        where[longest] = (where[longest] + shift) % array.shape[longest]
        spots.append(tuple(where))
    return array.at[spots[0]].set(smallest).at[spots[1]].set(top_value)


def levels(key, dims, shards, smallest, top_value):
    factor_of, own = 1.0, jax.random.fold_in(key, 6)
    for axis_at, parts in shards:
        draws = jnp.exp(jax.random.uniform(jax.random.fold_in(own, axis_at), (parts,), jnp.float32, smallest / len(shards), top_value / len(shards)))
        factor_of = factor_of * jnp.repeat(draws, dims[axis_at] // parts).reshape([-1 if axis == axis_at else 1 for axis in range(len(dims))])
    return factor_of


def noise(stream_key, dims, spread, bound, cuts=(), kind=jnp.bfloat16):
    entries = jax.random.normal(stream_key, dims, jnp.float32) * spread
    if len(cuts) > 0:
        entries = levels(stream_key, dims, cuts, -0.22, 0.18) * entries
    return jnp.clip(entries, min=-bound, max=bound).astype(kind)


def setup_inputs(seed: int = 0) -> dict:
    streams_of = jax.random.split(jax.random.key(seed), 7)
    noise_draws = noise(streams_of[0], (LEVELS, NODES, W, S), 1.0, 6.0, ((1, 16), (3, 16)))
    inverse_diagonal = draw_inverse_diagonal(jax.random.fold_in(streams_of[6], 71), 0)
    coupling_blocks = noise(streams_of[2], (LEVELS - 1, NODES, COUPLE, W, W), (2 * W * COUPLE) ** -0.5, 0.0625, ((1, 16), (2, 16)))
    ancestor_pick = place_ends(jax.random.randint(streams_of[3], (LEVELS - 1, OWNERS, OWNERS), 0, NODES_DEV), jax.random.fold_in(streams_of[3], 1), 0, NODES_DEV - 1).astype(jnp.int32)
    coupling_lists = draw_coupling_lists(jax.random.fold_in(streams_of[6], 71), 0)
    live_counts = draw_live_counts(jax.random.fold_in(streams_of[6], 71), 0)
    return {"noise_draws": noise_draws, "inverse_diagonal": inverse_diagonal, "coupling_blocks": coupling_blocks, "ancestor_pick": ancestor_pick, "coupling_lists": coupling_lists, "live_counts": live_counts}


def apply_inverse(inverse, right_side):
    product = jnp.einsum("nrc,nrs->ncs", inverse.astype(jnp.float32), right_side.astype(jnp.float32))
    return product.astype(jnp.bfloat16)


def reference(noise_draws, inverse_diagonal, coupling_blocks, ancestor_pick, coupling_lists, live_counts):
    owners = NODES // NODES_DEV
    node_owner = (jnp.arange(NODES) // NODES_DEV).astype(jnp.int32)
    levels_done = [apply_inverse(inverse_diagonal[0], noise_draws[0])]
    for level in range(1, LEVELS):
        known = jnp.concatenate(levels_done, axis=0)
        values = coupling_lists[level - 1]
        source_level = values // owners
        source_owner = values % owners
        local = ancestor_pick[source_level, node_owner[:, None], source_owner]
        rows_used = (source_level * NODES + source_owner * NODES_DEV + local).astype(jnp.int32)
        counts_here = live_counts[level - 1]
        blocks = coupling_blocks[level - 1]

        def turn(slot, total):
            picked = jnp.take(known, rows_used[:, slot], axis=0).astype(jnp.float32)
            alive = (slot < counts_here).astype(jnp.float32)
            block = lax.dynamic_index_in_dim(blocks, slot, 1, keepdims=False).astype(jnp.float32)
            return total + alive[:, None, None] * jnp.einsum("nrc,nrs->ncs", block, picked)

        updates = lax.fori_loop(0, COUPLE, turn, jnp.zeros(noise_draws.shape[1:], jnp.float32))
        right_side = (noise_draws[level].astype(jnp.float32) - updates).astype(jnp.bfloat16)
        levels_done.append(apply_inverse(inverse_diagonal[level], right_side))
    return jnp.stack(levels_done, axis=0)
```

```python
import jax
import jax.numpy as jnp
from jax import lax
from jax.experimental import pallas as pl
from jax.experimental.pallas import tpu as pltpu
from jax.sharding import PartitionSpec as P

MESH = pl.DeviceIdType.MESH
YS, ZS, XS, CORES = 4, 4, 4, 2
RING = 2 * ZS
DRAWS = 2 * XS * CORES
W = 256
F32, BF16 = jnp.float32, jnp.bfloat16


def kernel(pick, lists, counts, noise, inverse, blocks, out, *scratch):
    (noise_v, out_v, i0, i12, b1, b2, zrel, own0, own1, below, above, t0, t1, sb0, sb1, ry0, ry1, acc) = scratch[:18]
    (loc, inv_s, inv_r, zs, zr, xs, xr, xfs, xfr, cs, cr, ls, lr_b, lr_a, ys, yr, yfs, yfr, yrel) = scratch[18:]
    cols = own0.shape[1]
    half = cols // 2
    bf, own, table, send, relay = (b1, b2), (own0, own1), (t0, t1), (sb0, sb1), (ry0, ry1)
    below = (below[:3], below[3:])
    above = (above[:3], above[3:])

    leaf, draw = lax.axis_index("leaf"), lax.axis_index("draw")
    y, zl = lax.div(leaf, ZS), lax.rem(leaf, ZS)
    zh, q = lax.div(draw, XS * CORES), lax.rem(draw, XS * CORES)
    x, c = lax.div(q, CORES), lax.rem(q, CORES)
    z = zh * ZS + zl

    def at(y_, z_, x_, c_):
        return (y_ * ZS + lax.rem(z_, ZS), lax.div(z_, ZS) * (XS * CORES) + x_ * CORES + c_)

    def up(v, step, size):
        return lax.rem(v + step + size, size)

    north, south = at(up(y, 1, YS), z, x, c), at(up(y, -1, YS), z, x, c)
    z_up, z_down = at(y, up(z, 1, RING), x, c), at(y, up(z, -1, RING), x, c)
    z_up2, z_down2 = at(y, up(z, 2, RING), x, c), at(y, up(z, -2, RING), x, c)
    partner = at(y, up(z, ZS, RING), x, c)
    east, west = at(y, z, up(x, 1, XS), c), at(y, z, up(x, -1, XS), c)
    other = at(y, z, x, 1 - c)

    def slot(zh_, x_, c_):
        return zh_ * (XS * CORES) + x_ * CORES + c_

    pending = []

    def move(src, dst, s_sem, r_sem, device):
        return pltpu.make_async_remote_copy(
            src_ref=src, dst_ref=dst, send_sem=s_sem, recv_sem=r_sem, device_id=device, device_id_type=MESH
        )

    def put(*args, cond=None):
        if cond is None:
            move(*args).start()
        else:
            pl.when(cond)(lambda: move(*args).start())
        pending.append((args, cond))

    def got(dst, r_sem):
        move(dst, dst, r_sem, r_sem, east).wait_recv()

    def run(plan, cond=None):
        def body():
            for step in plan:
                if len(step) == 2:
                    got(*step)
                else:
                    move(*step).start()

        if cond is None:
            body()
        else:
            pl.when(cond)(body)
        pending.extend((step, cond) for step in plan if len(step) == 5)

    barrier = pltpu.get_barrier_semaphore()
    peers = [(leaf, zh * (XS * CORES) + lax.rem(q + j, XS * CORES)) for j in range(1, XS * CORES)]
    greeted = peers + [partner, z_up, z_down, z_up2, z_down2, north, south]
    noise_in = pltpu.make_async_copy(noise, noise_v, loc.at[0])
    noise_in.start()
    for device in greeted:
        pl.semaphore_signal(barrier, inc=1, device_id=device, device_id_type=MESH)
    pl.semaphore_wait(barrier, len(greeted))

    inv_dst = (
        lambda k: i0.at[:, pl.ds(pl.multiple_of(16 * k, 16), 16), :],
        lambda k: i12.at[:, :, pl.ds(pl.multiple_of(16 * k, 16), 16), :],
    )
    inv_src = (inverse.at[0], inverse.at[pl.ds(1, 2)])
    far = lax.rem(draw + XS * CORES, DRAWS)

    def inverse_first(g):
        put(inv_src[g], inv_dst[g](draw), inv_s.at[g, 0], inv_r.at[g, draw], partner)
        for j, device in enumerate(peers):
            put(inv_src[g], inv_dst[g](draw), inv_s.at[g, 1 + j], inv_r.at[g, draw], device)

    def inverse_next(g):
        got(inv_dst[g](far), inv_r.at[g, far])
        for j, device in enumerate(peers):
            put(inv_dst[g](far), inv_dst[g](far), inv_s.at[g, 8 + j], inv_r.at[g, far], device)

    def inverse_wait(g):
        for j in range(1, XS * CORES):
            for zz in (0, 1):
                k = zz * (XS * CORES) + lax.rem(q + j, XS * CORES)
                got(inv_dst[g](k), inv_r.at[g, k])

    inverse_own = [pltpu.make_async_copy(inv_src[g], inv_dst[g](draw), loc.at[1 + g]) for g in (0, 1)]
    blocks_own = [pltpu.make_async_copy(blocks.at[l, :, 0], bf[l].at[draw], loc.at[3 + l]) for l in (0, 1)]

    def blocks_z(l):
        put(blocks.at[l, 0, 0], zrel.at[l, 0], zs.at[l, 0], zr.at[l, 0], z_up2)
        put(blocks.at[l, 1, 0], zrel.at[l, 1], zs.at[l, 1], zr.at[l, 1], z_down2)

    def blocks_relay(l):
        k_up = slot(lax.div(up(z, -2, RING), ZS), x, c)
        k_down = slot(lax.div(up(z, 2, RING), ZS), x, c)
        got(zrel.at[l, 0], zr.at[l, 0])
        put(zrel.at[l, 0], bf[l].at[k_up, 0], zs.at[l, 2], zr.at[l, 2], z_up2)
        got(zrel.at[l, 1], zr.at[l, 1])
        put(zrel.at[l, 1], bf[l].at[k_down, 1], zs.at[l, 3], zr.at[l, 3], z_down2)

    def blocks_out(l, u):
        k = (draw, far)[u]
        src = blocks.at[l, :, 0] if u == 0 else bf[l].at[k]
        put(src, bf[l].at[k], xs.at[l, u, 0], xr.at[l, u, 0], east)
        put(src, bf[l].at[k], xs.at[l, u, 1], xr.at[l, u, 1], west)
        put(src, bf[l].at[k], cs.at[l, u, 0], cr.at[l, u, 0], other)

    def blocks_far(l):
        got(bf[l].at[far, 0], zr.at[l, 2])
        got(bf[l].at[far, 1], zr.at[l, 3])
        blocks_out(l, 1)

    def blocks_x(l, u):
        zz = zh if u == 0 else 1 - zh
        k_w, k_e = slot(zz, up(x, -1, XS), c), slot(zz, up(x, 1, XS), c)
        got(bf[l].at[k_w], xr.at[l, u, 0])
        put(bf[l].at[k_w, 0], bf[l].at[k_w, 0], xfs.at[l, u, 0], xfr.at[l, u, 0], east)
        put(bf[l].at[k_w], bf[l].at[k_w], cs.at[l, u, 1], cr.at[l, u, 1], other)
        got(bf[l].at[k_e], xr.at[l, u, 1])
        put(bf[l].at[k_e, 1], bf[l].at[k_e, 1], xfs.at[l, u, 1], xfr.at[l, u, 1], west)
        put(bf[l].at[k_e], bf[l].at[k_e], cs.at[l, u, 2], cr.at[l, u, 2], other)

    def blocks_x2(l, u):
        k = slot(zh if u == 0 else 1 - zh, up(x, 2, XS), c)
        for n in (0, 1):
            got(bf[l].at[k, n], xfr.at[l, u, n])
            put(bf[l].at[k, n], bf[l].at[k, n], cs.at[l, u, 3 + n], cr.at[l, u, 3 + n], other)

    def blocks_wait(l):
        for u in (0, 1):
            zz = zh if u == 0 else 1 - zh
            for i, step in enumerate((0, -1, 1)):
                k = slot(zz, up(x, step, XS), 1 - c)
                got(bf[l].at[k], cr.at[l, u, i])
            k = slot(zz, up(x, 2, XS), 1 - c)
            for n in (0, 1):
                got(bf[l].at[k, n], cr.at[l, u, 3 + n])
        blocks_own[l].wait()

    def choose(a, ref, s):
        src = y * ZS + s

        def wanted(step):
            return ref[pick[a, up(y, step, YS) * ZS + zl, src]]

        send[a][s, 0] = wanted(2)
        send[a][s, 1] = wanted(1)
        send[a][s, 2] = wanted(-1)
        table[a][src] = wanted(0)

    def send_y(a, s):
        src = y * ZS + s
        return [
            (send[a].at[s, 0, pl.ds(0, half)], relay[a].at[0, s], ys.at[a, s, 0], yrel.at[a, 0, s], north),
            (send[a].at[s, 0, pl.ds(half, half)], relay[a].at[1, s], ys.at[a, s, 1], yrel.at[a, 1, s], south),
            (send[a].at[s, 1], table[a].at[src], ys.at[a, s, 2], yr.at[a, 0, s], north),
            (send[a].at[s, 2], table[a].at[src], ys.at[a, s, 3], yr.at[a, 1, s], south),
        ]

    def pass_y(a, s):
        src0, src1 = up(y, -1, YS) * ZS + s, up(y, 1, YS) * ZS + s
        return [
            (relay[a].at[0, s], yrel.at[a, 0, s]),
            (relay[a].at[0, s], table[a].at[src0, pl.ds(0, half)], yfs.at[a, s, 0], yfr.at[a, 0, s], north),
            (relay[a].at[1, s], yrel.at[a, 1, s]),
            (relay[a].at[1, s], table[a].at[src1, pl.ds(half, half)], yfs.at[a, s, 1], yfr.at[a, 1, s], south),
        ]

    def arrived(a, s):
        got(table[a].at[up(y, -1, YS) * ZS + s], yr.at[a, 0, s])
        got(table[a].at[up(y, 1, YS) * ZS + s], yr.at[a, 1, s])
        k = up(y, 2, YS) * ZS + s
        got(table[a].at[k, pl.ds(0, half)], yfr.at[a, 0, s])
        got(table[a].at[k, pl.ds(half, half)], yfr.at[a, 1, s])

    def round_first(a):
        choose(a, own[a], zl)
        put(own[a], below[a][0], ls.at[a, 0, 0], lr_b.at[a, 0], z_up, cond=zl < ZS - 1)
        put(own[a], above[a][0], ls.at[a, 1, 0], lr_a.at[a, 0], z_down, cond=zl > 0)
        run(send_y(a, zl))

    def round_next(a, r):
        lines = (
            (below, lr_b, 0, z_up, zl >= r, zl < ZS - 1, zl - r),
            (above, lr_a, 1, z_down, zl <= ZS - 1 - r, zl > 0, zl + r),
        )
        for line, heard, way, device, here, more, s in lines:
            run([(line[a][r - 1], heard.at[a, r - 1])], here)
            if r < ZS - 1:
                put(
                    line[a][r - 1], line[a][r], ls.at[a, way, r], heard.at[a, r], device,
                    cond=jnp.logical_and(here, more),
                )
        for line, heard, way, device, here, more, s in lines:
            pl.when(here)(lambda line=line, s=s: choose(a, line[a][r - 1], s))
            run(send_y(a, s), here)

    def round_pass(a, r):
        if r == 0:
            run(pass_y(a, zl))
        else:
            run(pass_y(a, zl - r), zl >= r)
            run(pass_y(a, zl + r), zl <= ZS - 1 - r)

    def solve(level, right_side, n):
        inv = i0[n] if level == 0 else i12[level - 1, n]
        return jnp.dot(right_side, inv, preferred_element_type=F32).astype(BF16)

    def show(level, ref):
        for n in (0, 1):
            out_v[level, n] = ref[n].T
        copy = pltpu.make_async_copy(out_v.at[level], out.at[level], loc.at[5 + level])
        copy.start()
        return copy

    def add_slots(level, start, stop, source):
        @pl.loop(start, stop)
        def _(k):
            for n in (0, 1):
                alive = (k < counts[level, n]).astype(F32)
                values = source[lax.rem(lists[level, n, k], 16)]
                acc[n] += alive * jnp.dot(values, bf[level][k, n], preferred_element_type=F32)

    for copy in inverse_own + blocks_own:
        copy.start()
    inverse_first(0)
    blocks_z(0)
    noise_in.wait()
    flipped = [noise_v[0, n].T for n in (0, 1)]
    inverse_next(0)
    blocks_out(0, 0)
    inverse_own[0].wait()
    inverse_wait(0)
    for n in (0, 1):
        own0[n] = solve(0, flipped[n], n)
    round_first(0)
    inverse_first(1)
    blocks_relay(0)
    blocks_x(0, 0)
    blocks_far(0)
    shown = [show(0, own0)]
    round_next(0, 1)
    round_pass(0, 0)
    blocks_x(0, 1)
    blocks_x2(0, 0)
    inverse_next(1)
    round_next(0, 2)
    round_pass(0, 1)
    blocks_x2(0, 1)
    blocks_z(1)
    blocks_out(1, 0)
    round_next(0, 3)
    round_pass(0, 2)
    round_pass(0, 3)
    blocks_relay(1)
    blocks_wait(0)
    inverse_own[1].wait()
    inverse_wait(1)

    for n in (0, 1):
        acc[n] = jnp.zeros_like(acc[n])
    for s in range(ZS):
        arrived(0, s)
    add_slots(0, 0, 16, t0)
    for n in (0, 1):
        right_side = (noise_v[1, n].T.astype(F32) - acc[n]).astype(BF16)
        own1[n] = solve(1, right_side, n)
    round_first(1)
    blocks_x(1, 0)
    blocks_far(1)
    shown.append(show(1, own1))
    for n in (0, 1):
        acc[n] = jnp.zeros_like(acc[n])
    round_next(1, 1)
    round_pass(1, 0)
    blocks_x(1, 1)
    blocks_x2(1, 0)
    round_next(1, 2)
    round_pass(1, 1)
    blocks_x2(1, 1)
    round_next(1, 3)
    round_pass(1, 2)
    blocks_wait(1)
    add_slots(1, 8, 16, t0)
    round_pass(1, 3)

    for s in range(ZS):
        arrived(1, s)
    add_slots(1, 0, 8, t1)
    for n in (0, 1):
        right_side = (noise_v[2, n].T.astype(F32) - acc[n]).astype(BF16)
        out_v[2, n] = solve(2, right_side, n).T
    last = pltpu.make_async_copy(out_v.at[2], out.at[2], loc.at[7])
    last.start()
    for args, cond in pending:
        if cond is None:
            move(*args).wait_send()
        else:
            pl.when(cond)(lambda args=args: move(*args).wait_send())
    for copy in shown + [last]:
        copy.wait()


def on_device(noise_draws, inverse_diagonal, coupling_blocks, ancestor_pick, coupling_lists, live_counts):
    cols = noise_draws.shape[3]
    pair = pltpu.VMEM((2, cols, W), BF16)
    dma = pltpu.SemaphoreType.DMA
    scratch = [
        pltpu.VMEM(noise_draws.shape, BF16),
        pltpu.VMEM(noise_draws.shape, BF16),
        pltpu.VMEM((2, W, W), BF16),
        pltpu.VMEM((2, 2, W, W), BF16),
        pltpu.VMEM((DRAWS, 2, W, W), BF16),
        pltpu.VMEM((DRAWS, 2, W, W), BF16),
        pltpu.VMEM((2, 2, W, W), BF16),
        pair,
        pair,
        [pair] * 6,
        [pair] * 6,
        pltpu.VMEM((16, cols, W), BF16),
        pltpu.VMEM((16, cols, W), BF16),
        pltpu.VMEM((ZS, 3, cols, W), BF16),
        pltpu.VMEM((ZS, 3, cols, W), BF16),
        pltpu.VMEM((2, ZS, cols // 2, W), BF16),
        pltpu.VMEM((2, ZS, cols // 2, W), BF16),
        pltpu.VMEM((2, cols, W), F32),
        dma((8,)),
        dma((2, 16)),
        dma((2, 16)),
        dma((2, 4)),
        dma((2, 4)),
        dma((2, 2, 2)),
        dma((2, 2, 2)),
        dma((2, 2, 2)),
        dma((2, 2, 2)),
        dma((2, 2, 5)),
        dma((2, 2, 5)),
        dma((2, 2, 3)),
        dma((2, 3)),
        dma((2, 3)),
        dma((2, ZS, 4)),
        dma((2, 2, ZS)),
        dma((2, ZS, 2)),
        dma((2, 2, ZS)),
        dma((2, 2, ZS)),
    ]
    smem = pl.BlockSpec(memory_space=pltpu.SMEM)
    anywhere = pl.BlockSpec(memory_space=pl.ANY)
    return pl.pallas_call(
        kernel,
        out_shape=jax.ShapeDtypeStruct(noise_draws.shape, BF16),
        in_specs=[smem, smem, smem, anywhere, anywhere, anywhere],
        out_specs=anywhere,
        scratch_shapes=scratch,
        compiler_params=pltpu.CompilerParams(
            collective_id=0, has_side_effects=True, vmem_limit_bytes=60 * 1024 * 1024
        ),
    )(ancestor_pick, coupling_lists, live_counts, noise_draws, inverse_diagonal, coupling_blocks)


def solution(mesh):
    placed = (
        P(None, "leaf", None, "draw"),
        P(None, "leaf", "draw", None),
        P(None, "leaf", "draw", None, None),
        P(),
        P(None, "leaf", None),
        P(None, "leaf"),
    )
    return jax.shard_map(
        on_device,
        mesh=mesh,
        in_specs=placed,
        out_specs=P(None, "leaf", None, "draw"),
        check_vma=False,
    )
```

```python
import jax
import jax.numpy as jnp
from jax import lax
from jax.experimental import pallas as pl
from jax.experimental.pallas import tpu as pltpu
from jax.sharding import PartitionSpec as P

MESH = pl.DeviceIdType.MESH
YS, ZS, XS, CORES = 4, 4, 4, 2
RING = 2 * ZS
DRAWS = 2 * XS * CORES
OWNERS, SLOTS, W = 16, 16, 256
F32, BF16 = jnp.float32, jnp.bfloat16


def kernel(pick, lists, counts, noise, inverse, blocks, out_v, *scratch):
    (noise_v, flipped, i0, i12, b1, b2, zrel, own0, own1, below, above, t0, t1, sb0, sb1, ry0, ry1, acc, place) = scratch[:19]
    (loc, inv_s, inv_r, zs, zr, xs, xr, xfs, xfr, cs, cr, ls, lr, ys, yr, yrel) = scratch[19:]
    cols = own0.shape[1]
    half = cols // 2
    bf, own, table, send, relay = (b1, b2), (own0, own1), (t0, t1), (sb0, sb1), (ry0, ry1)

    leaf, draw = lax.axis_index("leaf"), lax.axis_index("draw")
    y, zl = lax.div(leaf, ZS), lax.rem(leaf, ZS)
    zh, q = lax.div(draw, XS * CORES), lax.rem(draw, XS * CORES)
    x, c = lax.div(q, CORES), lax.rem(q, CORES)
    z = zh * ZS + zl

    def at(y_, z_, x_, c_):
        return (y_ * ZS + lax.rem(z_, ZS), lax.div(z_, ZS) * (XS * CORES) + x_ * CORES + c_)

    def up(v, step, size):
        return lax.rem(v + step + size, size)

    north, south = at(up(y, 1, YS), z, x, c), at(up(y, -1, YS), z, x, c)
    z_up, z_down = at(y, up(z, 1, RING), x, c), at(y, up(z, -1, RING), x, c)
    z_up2, z_down2 = at(y, up(z, 2, RING), x, c), at(y, up(z, -2, RING), x, c)
    partner = at(y, up(z, ZS, RING), x, c)
    east, west = at(y, z, up(x, 1, XS), c), at(y, z, up(x, -1, XS), c)
    other = at(y, z, x, 1 - c)

    def slot(zh_, x_, c_):
        return zh_ * (XS * CORES) + x_ * CORES + c_

    pending = []

    def move(src, dst, s_sem, r_sem, device):
        return pltpu.make_async_remote_copy(
            src_ref=src, dst_ref=dst, send_sem=s_sem, recv_sem=r_sem, device_id=device, device_id_type=MESH
        )

    def put(*args, cond=None):
        if cond is None:
            move(*args).start()
        else:
            pl.when(cond)(lambda: move(*args).start())
        pending.append((args, cond))

    def got(dst, r_sem):
        move(dst, dst, r_sem, r_sem, east).wait_recv()

    def run(plan, cond=None):
        def body():
            for step in plan:
                if len(step) == 2:
                    got(*step)
                else:
                    move(*step).start()

        if cond is None:
            body()
        else:
            pl.when(cond)(body)
        pending.extend((step, cond) for step in plan if len(step) == 5)

    barrier = pltpu.get_barrier_semaphore()
    peers = [(leaf, zh * (XS * CORES) + lax.rem(q + j, XS * CORES)) for j in range(1, XS * CORES)]
    greeted = peers + [partner, z_up, z_down, z_up2, z_down2, north, south]
    noise_in = pltpu.make_async_copy(noise, noise_v, loc.at[0])
    noise_in.start()
    for device in greeted:
        pl.semaphore_signal(barrier, inc=1, device_id=device, device_id_type=MESH)
    pl.semaphore_wait(barrier, len(greeted))

    inv_dst = (
        lambda k: i0.at[:, pl.ds(pl.multiple_of(16 * k, 16), 16), :],
        lambda k: i12.at[:, :, pl.ds(pl.multiple_of(16 * k, 16), 16), :],
    )
    inv_src = (inverse.at[0], inverse.at[pl.ds(1, 2)])
    far = lax.rem(draw + XS * CORES, DRAWS)

    def inverse_across(g):
        put(inv_src[g], inv_dst[g](draw), inv_s.at[g, 0], inv_r.at[g, draw], partner)

    def inverse_first(g):
        for j, device in enumerate(peers):
            put(inv_src[g], inv_dst[g](draw), inv_s.at[g, 1 + j], inv_r.at[g, draw], device)

    def inverse_next(g):
        got(inv_dst[g](far), inv_r.at[g, far])
        for j, device in enumerate(peers):
            put(inv_dst[g](far), inv_dst[g](far), inv_s.at[g, 8 + j], inv_r.at[g, far], device)

    def inverse_wait(g):
        for j in range(1, XS * CORES):
            for zz in (0, 1):
                k = zz * (XS * CORES) + lax.rem(q + j, XS * CORES)
                got(inv_dst[g](k), inv_r.at[g, k])

    inverse_own = [pltpu.make_async_copy(inv_src[g], inv_dst[g](draw), loc.at[1 + g]) for g in (0, 1)]
    blocks_own = [pltpu.make_async_copy(blocks.at[l, :, 0], bf[l].at[draw], loc.at[3 + l]) for l in (0, 1)]

    def blocks_z(l):
        put(blocks.at[l, 0, 0], zrel.at[l, 0], zs.at[l, 0], zr.at[l, 0], z_up2)
        put(blocks.at[l, 1, 0], zrel.at[l, 1], zs.at[l, 1], zr.at[l, 1], z_down2)

    def blocks_relay(l):
        k_up = slot(lax.div(up(z, -2, RING), ZS), x, c)
        k_down = slot(lax.div(up(z, 2, RING), ZS), x, c)
        got(zrel.at[l, 0], zr.at[l, 0])
        put(zrel.at[l, 0], bf[l].at[k_up, 0], zs.at[l, 2], zr.at[l, 2], z_up2)
        got(zrel.at[l, 1], zr.at[l, 1])
        put(zrel.at[l, 1], bf[l].at[k_down, 1], zs.at[l, 3], zr.at[l, 3], z_down2)

    def blocks_out(l, u):
        k = (draw, far)[u]
        src = blocks.at[l, :, 0] if u == 0 else bf[l].at[k]
        put(src, bf[l].at[k], xs.at[l, u, 0], xr.at[l, u, 0], east)
        put(src, bf[l].at[k], xs.at[l, u, 1], xr.at[l, u, 1], west)
        put(src, bf[l].at[k], cs.at[l, u, 0], cr.at[l, u, 0], other)

    def blocks_far(l):
        got(bf[l].at[far, 0], zr.at[l, 2])
        got(bf[l].at[far, 1], zr.at[l, 3])
        blocks_out(l, 1)

    def blocks_x(l, u):
        zz = zh if u == 0 else 1 - zh
        k_w, k_e = slot(zz, up(x, -1, XS), c), slot(zz, up(x, 1, XS), c)
        got(bf[l].at[k_w], xr.at[l, u, 0])
        put(bf[l].at[k_w, 0], bf[l].at[k_w, 0], xfs.at[l, u, 0], xfr.at[l, u, 0], east)
        put(bf[l].at[k_w], bf[l].at[k_w], cs.at[l, u, 1], cr.at[l, u, 1], other)
        got(bf[l].at[k_e], xr.at[l, u, 1])
        put(bf[l].at[k_e, 1], bf[l].at[k_e, 1], xfs.at[l, u, 1], xfr.at[l, u, 1], west)
        put(bf[l].at[k_e], bf[l].at[k_e], cs.at[l, u, 2], cr.at[l, u, 2], other)

    def blocks_x2(l, u):
        k = slot(zh if u == 0 else 1 - zh, up(x, 2, XS), c)
        for n in (0, 1):
            got(bf[l].at[k, n], xfr.at[l, u, n])
            put(bf[l].at[k, n], bf[l].at[k, n], cs.at[l, u, 3 + n], cr.at[l, u, 3 + n], other)

    def blocks_wait(l):
        for u in (0, 1):
            zz = zh if u == 0 else 1 - zh
            for i, step in enumerate((0, -1, 1)):
                k = slot(zz, up(x, step, XS), 1 - c)
                got(bf[l].at[k], cr.at[l, u, i])
            k = slot(zz, up(x, 2, XS), 1 - c)
            for n in (0, 1):
                got(bf[l].at[k, n], cr.at[l, u, 3 + n])
        blocks_own[l].wait()

    def rows(h):
        return pl.ds(h * half, half)

    def choose(a, s, h, pair):
        src = y * ZS + s

        def wanted(step):
            return pair(pick[a, up(y, step, YS) * ZS + zl, src])

        send[a][s, 0, rows(h)] = wanted(2)
        send[a][s, 1, rows(h)] = wanted(1)
        send[a][s, 2, rows(h)] = wanted(-1)
        table[a][src, rows(h)] = wanted(0)

    def send_y(a, s, h):
        dst = table[a].at[y * ZS + s, rows(h)]
        far_way = (north, south)[h]
        return [
            (send[a].at[s, 0, rows(h)], relay[a].at[h, s], ys.at[a, s, h, 0], yrel.at[a, h, s], far_way),
            (send[a].at[s, 1, rows(h)], dst, ys.at[a, s, h, 1], yr.at[a, s, h, 0], north),
            (send[a].at[s, 2, rows(h)], dst, ys.at[a, s, h, 2], yr.at[a, s, h, 1], south),
        ]

    def pass_y(a, s, h):
        src = up(y, (-1, 1)[h], YS) * ZS + s
        return [
            (relay[a].at[h, s], yrel.at[a, h, s]),
            (relay[a].at[h, s], table[a].at[src, rows(h)], ys.at[a, s, h, 3], yr.at[a, s, h, 2], (north, south)[h]),
        ]

    def first(a, h):
        choose(a, zl, h, lambda n: own[a][n, rows(h)])
        put(own[a].at[:, rows(h)], below[a][0][h], ls.at[a, 0, 0, h], lr.at[a, 0, 0, h], z_up, cond=zl < ZS - 1)
        put(own[a].at[:, rows(h)], above[a][0][h], ls.at[a, 1, 0, h], lr.at[a, 1, 0, h], z_down, cond=zl > 0)
        run(send_y(a, zl, h))

    def follow(a, r, h):
        lines = (
            (below, 0, z_up, zl >= r, zl < ZS - 1, zl - r),
            (above, 1, z_down, zl <= ZS - 1 - r, zl > 0, zl + r),
        )
        for line, way, device, here, more, s in lines:
            run([(line[a][r - 1][h], lr.at[a, way, r - 1, h])], here)
            if r < ZS - 1:
                put(
                    line[a][r - 1][h], line[a][r][h], ls.at[a, way, r, h], lr.at[a, way, r, h], device,
                    cond=jnp.logical_and(here, more),
                )
        for line, way, device, here, more, s in lines:
            pl.when(here)(lambda line=line, s=s: choose(a, s, h, lambda n: line[a][r - 1][h][n]))
            run(send_y(a, s, h), here)

    def by_round(r, body):
        if r == 0:
            body(zl, None)
        else:
            body(zl - r, zl >= r)
            body(zl + r, zl <= ZS - 1 - r)

    def hand_on(a, r, h):
        by_round(r, lambda s, cond: run(pass_y(a, s, h), cond))

    def add_source(a, src):
        if a == 0:
            for n in (0, 1):
                k = place[0, n, src]
                alive = (k < counts[0, n]).astype(F32)
                acc[n] += alive * jnp.dot(t0[src], b1[k, n], preferred_element_type=F32)
        else:
            k = place[1, 0, src]
            second = place[1, 1, src]
            term = jnp.dot(t1[src], b2[k, second], preferred_element_type=F32)
            share = second.astype(F32)
            acc[0] += (1.0 - share) * term
            acc[1] += share * term

    def guarded(cond, body):
        if cond is None:
            body()
        else:
            pl.when(cond)(body)

    def use_near(a, r):
        def body(s, cond):
            def inner():
                add_source(a, y * ZS + s)
                for way, step in ((0, -1), (1, 1)):
                    src = up(y, step, YS) * ZS + s
                    for h in (0, 1):
                        got(table[a].at[src, rows(h)], yr.at[a, s, h, way])
                    add_source(a, src)

            guarded(cond, inner)

        by_round(r, body)

    def use_far(a, r):
        def body(s, cond):
            def inner():
                src = up(y, 2, YS) * ZS + s
                for h in (0, 1):
                    got(table[a].at[src, rows(h)], yr.at[a, s, h, 2])
                add_source(a, src)

            guarded(cond, inner)

        by_round(r, body)

    def find_places():
        @pl.loop(0, OWNERS)
        def _(o):
            zero = jnp.int32(0)
            for n in (0, 1):
                found = zero
                for k in range(SLOTS):
                    found = jnp.where(lists[0, n, k] == o, k, found)
                place[0, n, o] = found
            k0, n0 = zero, zero
            for k in range(SLOTS // 2):
                first_has, second_has = (lists[1, n, k] == OWNERS + o for n in (0, 1))
                k0 = jnp.where(jnp.logical_or(first_has, second_has), k, k0)
                n0 = jnp.where(second_has, 1, n0)
            place[1, 0, o], place[1, 1, o] = k0, n0

    def add_lower():
        @pl.loop(SLOTS // 2, SLOTS)
        def _(k):
            for n in (0, 1):
                alive = (k < counts[1, n]).astype(F32)
                values = t0[lax.rem(lists[1, n, k], OWNERS)]
                acc[n] += alive * jnp.dot(values, b2[k, n], preferred_element_type=F32)

    def solve(level, n, h):
        inv = i0[n] if level == 0 else i12[level - 1, n]
        right_side = flipped[level, n, rows(h)]
        if level > 0:
            right_side = (right_side.astype(F32) - acc[n, rows(h)]).astype(BF16)
        return jnp.dot(right_side, inv, preferred_element_type=F32).astype(BF16)

    def clear():
        for n in (0, 1):
            acc[n] = jnp.zeros_like(acc[n])

    def flip(level):
        for n in (0, 1):
            flipped[level, n] = noise_v[level, n].T

    def show(level, ref):
        for n in (0, 1):
            out_v[level, n] = ref[n].T

    def last(n, h):
        out_v[2, n, :, rows(h)] = solve(2, n, h).T

    def settle():
        for args, cond in pending:
            guarded(cond, lambda args=args: move(*args).wait_send())
        pending.clear()

    for copy in inverse_own + blocks_own:
        copy.start()
    inverse_across(0)
    inverse_first(0)
    inverse_across(1)
    blocks_z(0)
    noise_in.wait()
    flip(0)
    inverse_next(0)
    blocks_relay(0)
    inverse_own[0].wait()
    inverse_wait(0)
    for h in (0, 1):
        for n in (0, 1):
            own0[n, rows(h)] = solve(0, n, h)
        first(0, h)
    blocks_out(0, 0)
    find_places()
    inverse_first(1)
    follow(0, 1, 0)
    hand_on(0, 0, 0)
    blocks_x(0, 0)
    blocks_far(0)
    follow(0, 1, 1)
    hand_on(0, 0, 1)
    clear()
    flip(1)
    blocks_x2(0, 0)
    follow(0, 2, 0)
    blocks_x(0, 1)
    inverse_next(1)
    follow(0, 2, 1)
    hand_on(0, 1, 0)
    blocks_x2(0, 1)
    blocks_out(1, 0)
    hand_on(0, 1, 1)
    blocks_wait(0)
    use_near(0, 0)
    follow(0, 3, 0)
    hand_on(0, 2, 0)
    blocks_z(1)
    use_far(0, 0)
    use_near(0, 1)
    follow(0, 3, 1)
    hand_on(0, 2, 1)
    blocks_x(1, 0)
    hand_on(0, 3, 0)
    blocks_relay(1)
    use_far(0, 1)
    use_near(0, 2)
    hand_on(0, 3, 1)
    use_far(0, 2)
    inverse_own[1].wait()
    inverse_wait(1)
    blocks_x2(1, 0)
    use_near(0, 3)
    use_far(0, 3)

    for h in (0, 1):
        for n in (0, 1):
            own1[n, rows(h)] = solve(1, n, h)
        first(1, h)
    clear()
    show(0, own0)
    flip(2)
    follow(1, 1, 0)
    hand_on(1, 0, 0)
    show(1, own1)
    follow(1, 1, 1)
    hand_on(1, 0, 1)
    blocks_far(1)
    follow(1, 2, 0)
    follow(1, 2, 1)
    hand_on(1, 1, 0)
    blocks_x(1, 1)
    hand_on(1, 1, 1)
    follow(1, 3, 0)
    hand_on(1, 2, 0)
    blocks_x2(1, 1)
    blocks_wait(1)
    use_near(1, 0)
    follow(1, 3, 1)
    hand_on(1, 2, 1)
    use_far(1, 0)
    use_near(1, 1)
    hand_on(1, 3, 0)
    use_far(1, 1)
    use_near(1, 2)
    hand_on(1, 3, 1)
    add_lower()
    use_far(1, 2)
    settle()
    use_near(1, 3)
    use_far(1, 3)

    for n in (0, 1):
        for h in (0, 1):
            last(n, h)
    settle()


def on_device(noise_draws, inverse_diagonal, coupling_blocks, ancestor_pick, coupling_lists, live_counts):
    cols = noise_draws.shape[3]
    pair = pltpu.VMEM((2, cols, W), BF16)
    lines = [[[pltpu.VMEM((2, cols // 2, W), BF16)] * 2] * (ZS - 1)] * 2
    dma = pltpu.SemaphoreType.DMA
    scratch = [
        pltpu.VMEM(noise_draws.shape, BF16),
        pltpu.VMEM((3, 2, cols, W), BF16),
        pltpu.VMEM((2, W, W), BF16),
        pltpu.VMEM((2, 2, W, W), BF16),
        pltpu.VMEM((DRAWS, 2, W, W), BF16),
        pltpu.VMEM((DRAWS, 2, W, W), BF16),
        pltpu.VMEM((2, 2, W, W), BF16),
        pair,
        pair,
        lines,
        lines,
        pltpu.VMEM((16, cols, W), BF16),
        pltpu.VMEM((16, cols, W), BF16),
        pltpu.VMEM((ZS, 3, cols, W), BF16),
        pltpu.VMEM((ZS, 3, cols, W), BF16),
        pltpu.VMEM((2, ZS, cols // 2, W), BF16),
        pltpu.VMEM((2, ZS, cols // 2, W), BF16),
        pltpu.VMEM((2, cols, W), F32),
        pltpu.SMEM((2, 2, OWNERS), jnp.int32),
        dma((9,)),
        dma((2, 16)),
        dma((2, 16)),
        dma((2, 4)),
        dma((2, 4)),
        dma((2, 2, 2)),
        dma((2, 2, 2)),
        dma((2, 2, 2)),
        dma((2, 2, 2)),
        dma((2, 2, 5)),
        dma((2, 2, 5)),
        dma((2, 2, 3, 2)),
        dma((2, 2, 3, 2)),
        dma((2, ZS, 2, 4)),
        dma((2, ZS, 2, 3)),
        dma((2, 2, ZS)),
    ]
    smem = pl.BlockSpec(memory_space=pltpu.SMEM)
    anywhere = pl.BlockSpec(memory_space=pl.ANY)
    return pl.pallas_call(
        kernel,
        out_shape=pltpu.VMEM(noise_draws.shape, BF16),
        in_specs=[smem, smem, smem, anywhere, anywhere, anywhere],
        out_specs=pl.BlockSpec(memory_space=pltpu.VMEM),
        scratch_shapes=scratch,
        compiler_params=pltpu.CompilerParams(
            collective_id=0, has_side_effects=True, vmem_limit_bytes=60 * 1024 * 1024
        ),
    )(ancestor_pick, coupling_lists, live_counts, noise_draws, inverse_diagonal, coupling_blocks)


def solution(mesh):
    placed = (
        P(None, "leaf", None, "draw"),
        P(None, "leaf", "draw", None),
        P(None, "leaf", "draw", None, None),
        P(),
        P(None, "leaf", None),
        P(None, "leaf"),
    )
    return jax.shard_map(
        on_device,
        mesh=mesh,
        in_specs=placed,
        out_specs=P(None, "leaf", None, "draw"),
        check_vma=False,
    )
```

```python
import jax
import jax.numpy as jnp
from jax import lax
from jax.experimental import pallas as pl
from jax.experimental.pallas import tpu as pltpu
from jax.sharding import PartitionSpec as P

MESH = pl.DeviceIdType.MESH
YS, ZS, XS, CORES = 4, 4, 4, 2
RING = 2 * ZS
DRAWS = 2 * XS * CORES
LEVELS, OWNERS, SLOTS, W = 3, 16, 16, 256
F32, BF16 = jnp.float32, jnp.bfloat16


def kernel(pick, lists, counts, noise, inverse, blocks, out_v, *scratch):
    (noise_v, flipped, inv, b1, b2, zrel, own0, own1, below, above, t0, t1, sb0, sb1, ry0, ry1, acc, place) = scratch[:18]
    (loc, sent, inv_r, zr, xr, xfr, cr, lr, yr, yrel) = scratch[18:]
    cols = own0.shape[1]
    half = cols // 2
    bf, own, table, send, relay = (b1, b2), (own0, own1), (t0, t1), (sb0, sb1), (ry0, ry1)

    leaf, draw = lax.axis_index("leaf"), lax.axis_index("draw")
    y, zl = lax.div(leaf, ZS), lax.rem(leaf, ZS)
    zh, q = lax.div(draw, XS * CORES), lax.rem(draw, XS * CORES)
    x, c = lax.div(q, CORES), lax.rem(q, CORES)
    z = zh * ZS + zl

    def at(y_, z_, x_, c_):
        return (y_ * ZS + lax.rem(z_, ZS), lax.div(z_, ZS) * (XS * CORES) + x_ * CORES + c_)

    def up(v, step, size):
        return lax.rem(v + step + size, size)

    north, south = at(up(y, 1, YS), z, x, c), at(up(y, -1, YS), z, x, c)
    z_up, z_down = at(y, up(z, 1, RING), x, c), at(y, up(z, -1, RING), x, c)
    z_up2, z_down2 = at(y, up(z, 2, RING), x, c), at(y, up(z, -2, RING), x, c)
    partner = at(y, up(z, ZS, RING), x, c)
    east, west = at(y, z, up(x, 1, XS), c), at(y, z, up(x, -1, XS), c)
    other = at(y, z, x, 1 - c)

    def slot(zh_, x_, c_):
        return zh_ * (XS * CORES) + x_ * CORES + c_

    inside = jnp.logical_and(zl > 0, zl < ZS - 1)
    def move(src, dst, s_sem, r_sem, device):
        return pltpu.make_async_remote_copy(
            src_ref=src, dst_ref=dst, send_sem=s_sem, recv_sem=r_sem, device_id=device, device_id_type=MESH
        )

    def put(*args, cond=None):
        run([args], cond)

    def got(dst, r_sem):
        move(dst, dst, r_sem, r_sem, east).wait_recv()

    def left(group, region):
        move(region, region, sent.at[group], sent.at[group], east).wait_send()

    def run(plan, cond=None):
        def body():
            for step in plan:
                if len(step) == 2:
                    got(*step)
                else:
                    move(*step).start()

        if cond is None:
            body()
        else:
            pl.when(cond)(body)

    barrier = pltpu.get_barrier_semaphore()
    peers = [(leaf, zh * (XS * CORES) + lax.rem(q + j, XS * CORES)) for j in range(1, XS * CORES)]
    greeted = peers + [partner, z_up, z_down, z_up2, z_down2, north, south]
    noise_in = pltpu.make_async_copy(noise, noise_v, loc.at[0])
    noise_in.start()
    for device in greeted:
        pl.semaphore_signal(barrier, inc=1, device_id=device, device_id_type=MESH)
    pl.semaphore_wait(barrier, len(greeted))

    inv_dst = [
        lambda k, level=level: inv.at[level, :, pl.ds(pl.multiple_of(16 * k, 16), 16), :] for level in range(LEVELS)
    ]
    inv_src = [inverse.at[level] for level in range(LEVELS)]
    far = lax.rem(draw + XS * CORES, DRAWS)

    def inverse_across(g):
        put(inv_src[g], inv_dst[g](draw), sent.at[g], inv_r.at[g, 0], partner)

    def inverse_first(g):
        for device in peers:
            put(inv_src[g], inv_dst[g](draw), sent.at[g], inv_r.at[g, 1], device)

    def inverse_next(g):
        got(inv_dst[g](far), inv_r.at[g, 0])
        for device in peers:
            put(inv_dst[g](far), inv_dst[g](far), sent.at[g], inv_r.at[g, 1], device)

    def inverse_wait(g):
        got(inv.at[g, :, pl.ds(0, 224)], inv_r.at[g, 1])

    inverse_own = [pltpu.make_async_copy(inv_src[g], inv_dst[g](draw), loc.at[1 + g]) for g in range(LEVELS)]
    blocks_own = [pltpu.make_async_copy(blocks.at[l, :, 0], bf[l].at[draw], loc.at[4 + l]) for l in (0, 1)]

    def blocks_z(l):
        put(blocks.at[l, 0, 0], zrel.at[l, 0], sent.at[LEVELS + l], zr.at[l, 0], z_up2)
        put(blocks.at[l, 1, 0], zrel.at[l, 1], sent.at[LEVELS + l], zr.at[l, 1], z_down2)

    def blocks_relay(l, cond=None):
        k_up = slot(lax.div(up(z, -2, RING), ZS), x, c)
        k_down = slot(lax.div(up(z, 2, RING), ZS), x, c)
        plan = [
            (zrel.at[l, 0], zr.at[l, 0]),
            (zrel.at[l, 0], bf[l].at[k_up, 0], sent.at[LEVELS + l], zr.at[l, 2], z_up2),
            (zrel.at[l, 1], zr.at[l, 1]),
            (zrel.at[l, 1], bf[l].at[k_down, 1], sent.at[LEVELS + l], zr.at[l, 3], z_down2),
        ]
        run(plan, cond)

    def blocks_out(l, u):
        k = (draw, far)[u]
        src = blocks.at[l, :, 0] if u == 0 else bf[l].at[k]
        put(src, bf[l].at[k], sent.at[LEVELS + l], xr.at[l, u, 0], east)
        put(src, bf[l].at[k], sent.at[LEVELS + l], xr.at[l, u, 1], west)
        put(src, bf[l].at[k], sent.at[LEVELS + l], cr.at[l], other)

    def blocks_far(l):
        got(bf[l].at[far, 0], zr.at[l, 2])
        got(bf[l].at[far, 1], zr.at[l, 3])
        blocks_out(l, 1)

    def blocks_x(l, u):
        zz = zh if u == 0 else 1 - zh
        k_w, k_e = slot(zz, up(x, -1, XS), c), slot(zz, up(x, 1, XS), c)
        got(bf[l].at[k_w], xr.at[l, u, 0])
        put(bf[l].at[k_w, 0], bf[l].at[k_w, 0], sent.at[LEVELS + l], xfr.at[l, u, 0], east)
        put(bf[l].at[k_w], bf[l].at[k_w], sent.at[LEVELS + l], cr.at[l], other)
        got(bf[l].at[k_e], xr.at[l, u, 1])
        put(bf[l].at[k_e, 1], bf[l].at[k_e, 1], sent.at[LEVELS + l], xfr.at[l, u, 1], west)
        put(bf[l].at[k_e], bf[l].at[k_e], sent.at[LEVELS + l], cr.at[l], other)

    def blocks_x2(l, u):
        k = slot(zh if u == 0 else 1 - zh, up(x, 2, XS), c)
        for n in (0, 1):
            got(bf[l].at[k, n], xfr.at[l, u, n])
            put(bf[l].at[k, n], bf[l].at[k, n], sent.at[LEVELS + l], cr.at[l], other)

    def blocks_wait(l):
        got(bf[l].at[pl.ds(0, DRAWS // 2)], cr.at[l])
        blocks_own[l].wait()

    def parts(r):
        whole = [(0, half, 0), (half, half, 1)]
        return whole if r < ZS - 1 else whole[:1] + [(half, half // 2, 1), (half + half // 2, half // 2, 1)]

    def rows(part):
        return pl.ds(part[0], part[1])

    def relay_rows(part):
        return pl.ds(part[0] % half, part[1])

    def choose(a, s, part, pair):
        src = y * ZS + s

        def wanted(step):
            return pair(pick[a, up(y, step, YS) * ZS + zl, src])

        send[a][s, 0, rows(part)] = wanted(2)
        send[a][s, 1, rows(part)] = wanted(1)
        send[a][s, 2, rows(part)] = wanted(-1)
        table[a][src, rows(part)] = wanted(0)

    def send_y(a, s, i, part):
        dst = table[a].at[y * ZS + s, rows(part)]
        way = part[2]
        return [
            (
                send[a].at[s, 0, rows(part)], relay[a].at[way, s, relay_rows(part)], sent.at[LEVELS + 2 + a],
                yrel.at[a, i, s], (north, south)[way],
            ),
            (send[a].at[s, 1, rows(part)], dst, sent.at[LEVELS + 2 + a], yr.at[a, s, 0], north),
            (send[a].at[s, 2, rows(part)], dst, sent.at[LEVELS + 2 + a], yr.at[a, s, 1], south),
        ]

    def pass_y(a, s, i, part):
        way = part[2]
        src = up(y, (-1, 1)[way], YS) * ZS + s
        held = relay[a].at[way, s, relay_rows(part)]
        return [
            (held, yrel.at[a, i, s]),
            (held, table[a].at[src, rows(part)], sent.at[LEVELS + 2 + a], yr.at[a, s, 2], (north, south)[way]),
        ]

    def first(a, h):
        part = parts(0)[h]
        choose(a, zl, part, lambda n: own[a][n, rows(part)])
        put(own[a].at[:, rows(part)], below[a][0][h], sent.at[LEVELS + 4 + a], lr.at[a, 0, 0, h], z_up, cond=zl < ZS - 1)
        put(own[a].at[:, rows(part)], above[a][0][h], sent.at[LEVELS + 4 + a], lr.at[a, 1, 0, h], z_down, cond=zl > 0)
        run(send_y(a, zl, h, part))

    def follow(a, r, i):
        part = parts(r)[i]
        lines = (
            (below, 0, z_up, zl >= r, zl < ZS - 1, zl - r),
            (above, 1, z_down, zl <= ZS - 1 - r, zl > 0, zl + r),
        )
        for line, way, device, here, more, s in lines:
            held = line[a][r - 1][i]
            run([(held, lr.at[a, way, r - 1, i])], here)
            if r < ZS - 1:
                sends = []
                for j, (start, width, _) in enumerate(parts(r + 1)):
                    if part[0] <= start < part[0] + part[1]:
                        piece = held.at[:, pl.ds(start - part[0], width)]
                        sends.append((piece, line[a][r][j], sent.at[LEVELS + 4 + a], lr.at[a, way, r, j], device))
                run(sends, jnp.logical_and(here, more))
        for line, way, device, here, more, s in lines:
            pl.when(here)(lambda line=line, s=s: choose(a, s, part, lambda n: line[a][r - 1][i][n]))
            run(send_y(a, s, i, part), here)

    def by_round(r, body):
        if r == 0:
            body(zl, None)
        else:
            body(zl - r, zl >= r)
            body(zl + r, zl <= ZS - 1 - r)

    def hand_on(a, r, i):
        by_round(r, lambda s, cond: run(pass_y(a, s, i, parts(r)[i]), cond))

    def add_source(a, src):
        if a == 0:
            for n in (0, 1):
                k = place[0, n, src]
                alive = (k < counts[0, n]).astype(F32)
                acc[n] += alive * jnp.dot(t0[src], b1[k, n], preferred_element_type=F32)
        else:
            k = place[1, 0, src]
            second = place[1, 1, src]
            term = jnp.dot(t1[src], b2[k, second], preferred_element_type=F32)
            share = second.astype(F32)
            acc[0] += (1.0 - share) * term
            acc[1] += share * term

    def guarded(cond, body):
        if cond is None:
            body()
        else:
            pl.when(cond)(body)

    def use_near(a, r):
        def body(s, cond):
            def inner():
                add_source(a, y * ZS + s)
                for way, step in ((0, -1), (1, 1)):
                    src = up(y, step, YS) * ZS + s
                    got(table[a].at[src], yr.at[a, s, way])
                    add_source(a, src)

            guarded(cond, inner)

        by_round(r, body)

    def use_far(a, r):
        def body(s, cond):
            def inner():
                src = up(y, 2, YS) * ZS + s
                got(table[a].at[src], yr.at[a, s, 2])
                add_source(a, src)

            guarded(cond, inner)

        by_round(r, body)

    def find_places():
        @pl.loop(0, OWNERS)
        def _(o):
            zero = jnp.int32(0)
            for n in (0, 1):
                found = zero
                for k in range(SLOTS):
                    found = jnp.where(lists[0, n, k] == o, k, found)
                place[0, n, o] = found
            k0, n0 = zero, zero
            for k in range(SLOTS // 2):
                first_has, second_has = (lists[1, n, k] == OWNERS + o for n in (0, 1))
                k0 = jnp.where(jnp.logical_or(first_has, second_has), k, k0)
                n0 = jnp.where(second_has, 1, n0)
            place[1, 0, o], place[1, 1, o] = k0, n0

    def add_lower():
        @pl.loop(SLOTS // 2, SLOTS)
        def _(k):
            for n in (0, 1):
                alive = (k < counts[1, n]).astype(F32)
                values = t0[lax.rem(lists[1, n, k], OWNERS)]
                acc[n] += alive * jnp.dot(values, b2[k, n], preferred_element_type=F32)

    def solve(level, n, part):
        right_side = flipped[level, n, rows(part)]
        if level > 0:
            right_side = (right_side.astype(F32) - acc[n, rows(part)]).astype(BF16)
        return jnp.dot(right_side, inv[level, n], preferred_element_type=F32).astype(BF16)

    def clear():
        for n in (0, 1):
            acc[n] = jnp.zeros_like(acc[n])

    def flip(level):
        for n in (0, 1):
            flipped[level, n] = noise_v[level, n].T

    def show(level, ref):
        for n in (0, 1):
            out_v[level, n] = ref[n].T

    def last(n):
        out_v[2, n] = solve(2, n, (0, cols)).T

    def settle(a):
        left(a, inv.at[a, :, pl.ds(0, 240)])
        left(LEVELS + a, table[a])
        left(LEVELS + 2 + a, table[a])
        pl.when(inside)(lambda: left(LEVELS + 4 + a, table[a].at[pl.ds(0, 10)]))
        pl.when(jnp.logical_not(inside))(lambda: left(LEVELS + 4 + a, table[a].at[pl.ds(0, 2)]))

    for copy in inverse_own + blocks_own:
        copy.start()
    inverse_across(0)
    inverse_first(0)
    blocks_z(0)
    inverse_across(1)
    noise_in.wait()
    flip(0)
    inverse_next(0)
    blocks_relay(0)
    inverse_own[0].wait()
    inverse_wait(0)
    for h in (0, 1):
        for n in (0, 1):
            own0[n, rows(parts(0)[h])] = solve(0, n, parts(0)[h])
        first(0, h)
    blocks_out(0, 0)
    find_places()
    inverse_first(1)
    follow(0, 1, 0)
    hand_on(0, 0, 0)
    blocks_x(0, 0)
    blocks_far(0)
    follow(0, 1, 1)
    hand_on(0, 0, 1)
    clear()
    flip(1)
    blocks_x2(0, 0)
    follow(0, 2, 0)
    blocks_x(0, 1)
    inverse_next(1)
    follow(0, 2, 1)
    hand_on(0, 1, 0)
    blocks_x2(0, 1)
    blocks_out(1, 0)
    hand_on(0, 1, 1)
    blocks_wait(0)
    use_near(0, 0)
    follow(0, 3, 0)
    hand_on(0, 2, 0)
    use_far(0, 0)
    follow(0, 3, 1)
    use_near(0, 1)
    hand_on(0, 2, 1)
    follow(0, 3, 2)
    blocks_z(1)
    blocks_x(1, 0)
    hand_on(0, 3, 0)
    blocks_relay(1, inside)
    use_far(0, 1)
    use_near(0, 2)
    hand_on(0, 3, 1)
    hand_on(0, 3, 2)
    blocks_relay(1, jnp.logical_not(inside))
    use_far(0, 2)
    inverse_own[1].wait()
    inverse_wait(1)
    blocks_x2(1, 0)
    use_near(0, 3)
    use_far(0, 3)

    for h in (0, 1):
        for n in (0, 1):
            own1[n, rows(parts(0)[h])] = solve(1, n, parts(0)[h])
        first(1, h)
    clear()
    show(0, own0)
    flip(2)
    follow(1, 1, 0)
    hand_on(1, 0, 0)
    show(1, own1)
    follow(1, 1, 1)
    hand_on(1, 0, 1)
    follow(1, 2, 0)
    blocks_far(1)
    inverse_across(2)
    inverse_first(2)
    follow(1, 2, 1)
    hand_on(1, 1, 0)
    blocks_x(1, 1)
    hand_on(1, 1, 1)
    follow(1, 3, 0)
    hand_on(1, 2, 0)
    blocks_x2(1, 1)
    blocks_wait(1)
    add_lower()
    settle(0)
    follow(1, 3, 1)
    hand_on(1, 2, 1)
    use_near(1, 0)
    use_far(1, 0)
    follow(1, 3, 2)
    use_near(1, 1)
    hand_on(1, 3, 0)
    inverse_next(2)
    use_far(1, 1)
    use_near(1, 2)
    hand_on(1, 3, 1)
    hand_on(1, 3, 2)
    use_far(1, 2)
    use_near(1, 3)
    inverse_own[2].wait()
    inverse_wait(2)
    use_far(1, 3)

    for n in (0, 1):
        last(n)
    settle(1)
    left(2, inv.at[2, :, pl.ds(0, 240)])


def on_device(noise_draws, inverse_diagonal, coupling_blocks, ancestor_pick, coupling_lists, live_counts):
    cols = noise_draws.shape[3]
    pair = pltpu.VMEM((2, cols, W), BF16)
    whole, fine = (pltpu.VMEM((2, width, W), BF16) for width in (cols // 2, cols // 4))
    lines = [[[whole] * 2] * (ZS - 2) + [[whole, fine, fine]]] * 2
    dma = pltpu.SemaphoreType.DMA
    scratch = [
        pltpu.VMEM(noise_draws.shape, BF16),
        pltpu.VMEM((3, 2, cols, W), BF16),
        pltpu.VMEM((LEVELS, 2, W, W), BF16),
        pltpu.VMEM((DRAWS, 2, W, W), BF16),
        pltpu.VMEM((DRAWS, 2, W, W), BF16),
        pltpu.VMEM((2, 2, W, W), BF16),
        pair,
        pair,
        lines,
        lines,
        pltpu.VMEM((16, cols, W), BF16),
        pltpu.VMEM((16, cols, W), BF16),
        pltpu.VMEM((ZS, 3, cols, W), BF16),
        pltpu.VMEM((ZS, 3, cols, W), BF16),
        pltpu.VMEM((2, ZS, cols // 2, W), BF16),
        pltpu.VMEM((2, ZS, cols // 2, W), BF16),
        pltpu.VMEM((2, cols, W), F32),
        pltpu.SMEM((2, 2, OWNERS), jnp.int32),
        dma((6,)),
        dma((LEVELS + 6,)),
        dma((LEVELS, 2)),
        dma((2, 4)),
        dma((2, 2, 2)),
        dma((2, 2, 2)),
        dma((2,)),
        dma((2, 2, 3, 3)),
        dma((2, ZS, 3)),
        dma((2, 3, ZS)),
    ]
    smem = pl.BlockSpec(memory_space=pltpu.SMEM)
    anywhere = pl.BlockSpec(memory_space=pl.ANY)
    return pl.pallas_call(
        kernel,
        out_shape=pltpu.VMEM(noise_draws.shape, BF16),
        in_specs=[smem, smem, smem, anywhere, anywhere, anywhere],
        out_specs=pl.BlockSpec(memory_space=pltpu.VMEM),
        scratch_shapes=scratch,
        compiler_params=pltpu.CompilerParams(
            collective_id=0, has_side_effects=True, vmem_limit_bytes=60 * 1024 * 1024
        ),
    )(ancestor_pick, coupling_lists, live_counts, noise_draws, inverse_diagonal, coupling_blocks)


def solution(mesh):
    placed = (
        P(None, "leaf", None, "draw"),
        P(None, "leaf", "draw", None),
        P(None, "leaf", "draw", None, None),
        P(),
        P(None, "leaf", None),
        P(None, "leaf"),
    )
    return jax.shard_map(
        on_device,
        mesh=mesh,
        in_specs=placed,
        out_specs=P(None, "leaf", None, "draw"),
        check_vma=False,
    )
```

```python
import jax
import jax.numpy as jnp
from jax import lax
from jax.experimental import pallas as pl
from jax.experimental.pallas import tpu as pltpu
from jax.sharding import PartitionSpec as P

MESH = pl.DeviceIdType.MESH
YS, ZS, XS, CORES = 4, 4, 4, 2
RING = 2 * ZS
DRAWS = 2 * XS * CORES
LEVELS, OWNERS, SLOTS, W = 3, 16, 16, 256
F32, BF16 = jnp.float32, jnp.bfloat16


def kernel(pick, lists, counts, noise, inverse, blocks, out_v, *scratch):
    (noise_v, flipped, inv, b1, b2, zrel, own0, own1, below, above, t0, t1, sb0, sb1, ry0, ry1, acc, place) = scratch[:18]
    (loc, sent, inv_r, zr, xr, xfr, cr, lr, yr, yrel) = scratch[18:]
    cols = own0.shape[1]
    half = cols // 2
    bf, own, table, send, relay = (b1, b2), (own0, own1), (t0, t1), (sb0, sb1), (ry0, ry1)

    leaf, draw = lax.axis_index("leaf"), lax.axis_index("draw")
    y, zl = lax.div(leaf, ZS), lax.rem(leaf, ZS)
    zh, q = lax.div(draw, XS * CORES), lax.rem(draw, XS * CORES)
    x, c = lax.div(q, CORES), lax.rem(q, CORES)
    z = zh * ZS + zl

    def at(y_, z_, x_, c_):
        return (y_ * ZS + lax.rem(z_, ZS), lax.div(z_, ZS) * (XS * CORES) + x_ * CORES + c_)

    def up(v, step, size):
        return lax.rem(v + step + size, size)

    north, south = at(up(y, 1, YS), z, x, c), at(up(y, -1, YS), z, x, c)
    z_up, z_down = at(y, up(z, 1, RING), x, c), at(y, up(z, -1, RING), x, c)
    z_up2, z_down2 = at(y, up(z, 2, RING), x, c), at(y, up(z, -2, RING), x, c)
    partner = at(y, up(z, ZS, RING), x, c)
    east, west = at(y, z, up(x, 1, XS), c), at(y, z, up(x, -1, XS), c)
    other = at(y, z, x, 1 - c)

    def slot(zh_, x_, c_):
        return zh_ * (XS * CORES) + x_ * CORES + c_

    inside = jnp.logical_and(zl > 0, zl < ZS - 1)
    outside = jnp.logical_not(inside)
    def move(src, dst, s_sem, r_sem, device):
        return pltpu.make_async_remote_copy(
            src_ref=src, dst_ref=dst, send_sem=s_sem, recv_sem=r_sem, device_id=device, device_id_type=MESH
        )

    def put(*args, cond=None):
        run([args], cond)

    def got(dst, r_sem):
        move(dst, dst, r_sem, r_sem, east).wait_recv()

    def left(group, region):
        move(region, region, sent.at[group], sent.at[group], east).wait_send()

    def run(plan, cond=None):
        def body():
            for step in plan:
                if len(step) == 2:
                    got(*step)
                else:
                    move(*step).start()

        if cond is None:
            body()
        else:
            pl.when(cond)(body)

    barrier = pltpu.get_barrier_semaphore()
    peers = [(leaf, zh * (XS * CORES) + lax.rem(q + j, XS * CORES)) for j in range(1, XS * CORES)]
    greeted = peers + [partner, z_up, z_down, z_up2, z_down2, north, south]
    noise_in = pltpu.make_async_copy(noise, noise_v, loc.at[0])
    noise_in.start()
    for device in greeted:
        pl.semaphore_signal(barrier, inc=1, device_id=device, device_id_type=MESH)
    pl.semaphore_wait(barrier, len(greeted))

    inv_dst = [
        lambda k, level=level: inv.at[level, :, pl.ds(pl.multiple_of(16 * k, 16), 16), :] for level in range(LEVELS)
    ]
    inv_src = [inverse.at[level] for level in range(LEVELS)]
    far = lax.rem(draw + XS * CORES, DRAWS)

    def inverse_across(g):
        put(inv_src[g], inv_dst[g](draw), sent.at[g], inv_r.at[g, 0], partner)

    def inverse_first(g):
        for device in peers:
            put(inv_src[g], inv_dst[g](draw), sent.at[g], inv_r.at[g, 1], device)

    def inverse_next(g):
        got(inv_dst[g](far), inv_r.at[g, 0])
        for device in peers:
            put(inv_dst[g](far), inv_dst[g](far), sent.at[g], inv_r.at[g, 1], device)

    def inverse_wait(g):
        got(inv.at[g, :, pl.ds(0, 224)], inv_r.at[g, 1])

    inverse_own = [pltpu.make_async_copy(inv_src[g], inv_dst[g](draw), loc.at[1 + g]) for g in range(LEVELS)]
    blocks_own = [pltpu.make_async_copy(blocks.at[l, :, 0], bf[l].at[draw], loc.at[4 + l]) for l in (0, 1)]

    def blocks_z(l, cond=None):
        plan = [
            (blocks.at[l, 0, 0], zrel.at[l, 0], sent.at[LEVELS + l], zr.at[l, 0], z_up2),
            (blocks.at[l, 1, 0], zrel.at[l, 1], sent.at[LEVELS + l], zr.at[l, 1], z_down2),
        ]
        run(plan, cond)

    def blocks_relay(l, cond=None):
        k_up = slot(lax.div(up(z, -2, RING), ZS), x, c)
        k_down = slot(lax.div(up(z, 2, RING), ZS), x, c)
        plan = [
            (zrel.at[l, 0], zr.at[l, 0]),
            (zrel.at[l, 0], bf[l].at[k_up, 0], sent.at[LEVELS + l], zr.at[l, 2], z_up2),
            (zrel.at[l, 1], zr.at[l, 1]),
            (zrel.at[l, 1], bf[l].at[k_down, 1], sent.at[LEVELS + l], zr.at[l, 3], z_down2),
        ]
        run(plan, cond)

    def blocks_out(l, u):
        k = (draw, far)[u]
        src = blocks.at[l, :, 0] if u == 0 else bf[l].at[k]
        put(src, bf[l].at[k], sent.at[LEVELS + l], xr.at[l, u, 0], east)
        put(src, bf[l].at[k], sent.at[LEVELS + l], xr.at[l, u, 1], west)
        put(src, bf[l].at[k], sent.at[LEVELS + l], cr.at[l], other)

    def blocks_far(l):
        got(bf[l].at[far, 0], zr.at[l, 2])
        got(bf[l].at[far, 1], zr.at[l, 3])
        blocks_out(l, 1)

    def blocks_x(l, u):
        zz = zh if u == 0 else 1 - zh
        k_w, k_e = slot(zz, up(x, -1, XS), c), slot(zz, up(x, 1, XS), c)
        got(bf[l].at[k_w], xr.at[l, u, 0])
        put(bf[l].at[k_w, 0], bf[l].at[k_w, 0], sent.at[LEVELS + l], xfr.at[l, u, 0], east)
        put(bf[l].at[k_w], bf[l].at[k_w], sent.at[LEVELS + l], cr.at[l], other)
        got(bf[l].at[k_e], xr.at[l, u, 1])
        put(bf[l].at[k_e, 1], bf[l].at[k_e, 1], sent.at[LEVELS + l], xfr.at[l, u, 1], west)
        put(bf[l].at[k_e], bf[l].at[k_e], sent.at[LEVELS + l], cr.at[l], other)

    def blocks_x2(l, u):
        k = slot(zh if u == 0 else 1 - zh, up(x, 2, XS), c)
        for n in (0, 1):
            got(bf[l].at[k, n], xfr.at[l, u, n])
            put(bf[l].at[k, n], bf[l].at[k, n], sent.at[LEVELS + l], cr.at[l], other)

    def blocks_wait(l):
        got(bf[l].at[pl.ds(0, DRAWS // 2)], cr.at[l])
        blocks_own[l].wait()

    def parts(r):
        whole = [(0, half, 0), (half, half, 1)]
        return whole if r < ZS - 1 else whole[:1] + [(half, half // 2, 1), (half + half // 2, half // 2, 1)]

    def rows(part):
        return pl.ds(part[0], part[1])

    def relay_rows(part):
        return pl.ds(part[0] % half, part[1])

    def choose(a, s, part, pair):
        src = y * ZS + s

        def wanted(step):
            return pair(pick[a, up(y, step, YS) * ZS + zl, src])

        send[a][s, 0, rows(part)] = wanted(2)
        send[a][s, 1, rows(part)] = wanted(1)
        send[a][s, 2, rows(part)] = wanted(-1)
        table[a][src, rows(part)] = wanted(0)

    def send_far(a, s, i, part):
        way = part[2]
        return [(
            send[a].at[s, 0, rows(part)], relay[a].at[way, s, relay_rows(part)], sent.at[LEVELS + 2 + a],
            yrel.at[a, i, s], (north, south)[way],
        )]

    def send_near(a, s, part):
        dst = table[a].at[y * ZS + s, rows(part)]
        return [
            (send[a].at[s, 1, rows(part)], dst, sent.at[LEVELS + 2 + a], yr.at[a, s, 0], north),
            (send[a].at[s, 2, rows(part)], dst, sent.at[LEVELS + 2 + a], yr.at[a, s, 1], south),
        ]

    def pass_y(a, s, i, part):
        way = part[2]
        src = up(y, (-1, 1)[way], YS) * ZS + s
        held = relay[a].at[way, s, relay_rows(part)]
        return [
            (held, yrel.at[a, i, s]),
            (held, table[a].at[src, rows(part)], sent.at[LEVELS + 2 + a], yr.at[a, s, 2], (north, south)[way]),
        ]

    def first(a, h):
        part = parts(0)[h]
        choose(a, zl, part, lambda n: own[a][n, rows(part)])
        put(own[a].at[:, rows(part)], below[a][0][h], sent.at[LEVELS + 4 + a], lr.at[a, 0, 0, h], z_up, cond=zl < ZS - 1)
        put(own[a].at[:, rows(part)], above[a][0][h], sent.at[LEVELS + 4 + a], lr.at[a, 1, 0, h], z_down, cond=zl > 0)
        run(send_far(a, zl, h, part) + send_near(a, zl, part))

    def follow(a, r, i):
        part = parts(r)[i]
        lines = (
            (below, 0, z_up, zl >= r, zl < ZS - 1, zl - r),
            (above, 1, z_down, zl <= ZS - 1 - r, zl > 0, zl + r),
        )
        for line, way, device, here, more, s in lines:
            held = line[a][r - 1][i]
            run([(held, lr.at[a, way, r - 1, i])], here)
            if r < ZS - 1:
                sends = []
                for j, (start, width, _) in enumerate(parts(r + 1)):
                    if part[0] <= start < part[0] + part[1]:
                        piece = held.at[:, pl.ds(start - part[0], width)]
                        sends.append((piece, line[a][r][j], sent.at[LEVELS + 4 + a], lr.at[a, way, r, j], device))
                run(sends, jnp.logical_and(here, more))
        for line, way, device, here, more, s in lines:
            pl.when(here)(lambda line=line, s=s: choose(a, s, part, lambda n: line[a][r - 1][i][n]))
            run(send_far(a, s, i, part), here)
        ready = {(ZS - 1, 1): [], (ZS - 1, 2): parts(r)[1:]}.get((r, i), [part])
        for line, way, device, here, more, s in lines:
            run([step for each in ready for step in send_near(a, s, each)], here)

    def both(cond, only):
        return cond if only is None else only if cond is None else jnp.logical_and(cond, only)

    def by_round(r, body, only):
        if r == 0:
            body(zl, only)
        else:
            body(zl - r, both(zl >= r, only))
            body(zl + r, both(zl <= ZS - 1 - r, only))

    def hand_on(a, r, i, only=None):
        by_round(r, lambda s, cond: run(pass_y(a, s, i, parts(r)[i]), cond), only)

    def add_source(a, src):
        if a == 0:
            for n in (0, 1):
                k = place[0, n, src]
                alive = (k < counts[0, n]).astype(F32)
                acc[n] += alive * jnp.dot(t0[src], b1[k, n], preferred_element_type=F32)
        else:
            k = place[1, 0, src]
            second = place[1, 1, src]
            term = jnp.dot(t1[src], b2[k, second], preferred_element_type=F32)
            share = second.astype(F32)
            acc[0] += (1.0 - share) * term
            acc[1] += share * term

    def guarded(cond, body):
        if cond is None:
            body()
        else:
            pl.when(cond)(body)

    def use_near(a, r, only=None):
        def body(s, cond):
            def inner():
                add_source(a, y * ZS + s)
                for way, step in ((0, -1), (1, 1)):
                    src = up(y, step, YS) * ZS + s
                    got(table[a].at[src], yr.at[a, s, way])
                    add_source(a, src)

            guarded(cond, inner)

        by_round(r, body, only)

    def use_far(a, r, only=None):
        def body(s, cond):
            def inner():
                src = up(y, 2, YS) * ZS + s
                got(table[a].at[src], yr.at[a, s, 2])
                add_source(a, src)

            guarded(cond, inner)

        by_round(r, body, only)

    def find_places():
        @pl.loop(0, OWNERS)
        def _(o):
            zero = jnp.int32(0)
            for n in (0, 1):
                found = zero
                for k in range(SLOTS):
                    found = jnp.where(lists[0, n, k] == o, k, found)
                place[0, n, o] = found
            k0, n0 = zero, zero
            for k in range(SLOTS // 2):
                first_has, second_has = (lists[1, n, k] == OWNERS + o for n in (0, 1))
                k0 = jnp.where(jnp.logical_or(first_has, second_has), k, k0)
                n0 = jnp.where(second_has, 1, n0)
            place[1, 0, o], place[1, 1, o] = k0, n0

    def add_lower():
        @pl.loop(SLOTS // 2, SLOTS)
        def _(k):
            for n in (0, 1):
                alive = (k < counts[1, n]).astype(F32)
                values = t0[lax.rem(lists[1, n, k], OWNERS)]
                acc[n] += alive * jnp.dot(values, b2[k, n], preferred_element_type=F32)

    def solve(level, n, part):
        right_side = flipped[level, n, rows(part)]
        if level > 0:
            right_side = (right_side.astype(F32) - acc[n, rows(part)]).astype(BF16)
        return jnp.dot(right_side, inv[level, n], preferred_element_type=F32).astype(BF16)

    def clear():
        for n in (0, 1):
            acc[n] = jnp.zeros_like(acc[n])

    def flip(level):
        for n in (0, 1):
            flipped[level, n] = noise_v[level, n].T

    def show(level, ref):
        for n in (0, 1):
            out_v[level, n] = ref[n].T

    def last(n):
        out_v[2, n] = solve(2, n, (0, cols)).T

    def settle(a):
        left(a, inv.at[a, :, pl.ds(0, 240)])
        left(LEVELS + a, table[a])
        left(LEVELS + 2 + a, table[a])
        pl.when(inside)(lambda: left(LEVELS + 4 + a, table[a].at[pl.ds(0, 10)]))
        pl.when(outside)(lambda: left(LEVELS + 4 + a, table[a].at[pl.ds(0, 2)]))

    for copy in inverse_own + blocks_own:
        copy.start()
    inverse_across(0)
    inverse_first(0)
    blocks_z(0)
    inverse_across(1)
    noise_in.wait()
    flip(0)
    inverse_next(0)
    blocks_relay(0)
    inverse_own[0].wait()
    inverse_wait(0)
    for h in (0, 1):
        for n in (0, 1):
            own0[n, rows(parts(0)[h])] = solve(0, n, parts(0)[h])
        first(0, h)
    blocks_out(0, 0)
    find_places()
    inverse_first(1)
    hand_on(0, 0, 0)
    hand_on(0, 0, 1)
    follow(0, 1, 0)
    blocks_x(0, 0)
    blocks_far(0)
    follow(0, 1, 1)
    hand_on(0, 1, 0, outside)
    clear()
    flip(1)
    blocks_x2(0, 0)
    follow(0, 2, 0)
    hand_on(0, 1, 0, inside)
    blocks_x(0, 1)
    hand_on(0, 1, 1, outside)
    inverse_next(1)
    follow(0, 2, 1)
    hand_on(0, 1, 1, inside)
    blocks_x2(0, 1)
    blocks_out(1, 0)
    blocks_z(1, outside)
    hand_on(0, 2, 0, outside)
    blocks_wait(0)
    use_near(0, 0, outside)
    hand_on(0, 2, 0, inside)
    follow(0, 3, 0)
    hand_on(0, 2, 1)
    use_near(0, 0, inside)
    use_far(0, 0)
    follow(0, 3, 1)
    use_near(0, 1)
    follow(0, 3, 2)
    blocks_z(1, inside)
    hand_on(0, 3, 0)
    blocks_x(1, 0)
    use_far(0, 1)
    blocks_relay(1, inside)
    hand_on(0, 3, 1)
    use_near(0, 2)
    hand_on(0, 3, 2)
    use_far(0, 2)
    inverse_own[1].wait()
    inverse_wait(1)
    blocks_x2(1, 0)
    use_near(0, 3)
    use_far(0, 3)

    for h in (0, 1):
        for n in (0, 1):
            own1[n, rows(parts(0)[h])] = solve(1, n, parts(0)[h])
        first(1, h)
    blocks_relay(1, outside)
    clear()
    show(0, own0)
    flip(2)
    hand_on(1, 0, 0)
    hand_on(1, 0, 1)
    follow(1, 1, 0)
    show(1, own1)
    follow(1, 1, 1)
    hand_on(1, 1, 0, outside)
    follow(1, 2, 0)
    hand_on(1, 1, 0, inside)
    hand_on(1, 1, 1, outside)
    blocks_far(1)
    inverse_across(2)
    inverse_first(2)
    follow(1, 2, 1)
    hand_on(1, 1, 1, inside)
    blocks_x(1, 1)
    hand_on(1, 2, 0)
    follow(1, 3, 0)
    hand_on(1, 2, 1)
    blocks_x2(1, 1)
    blocks_wait(1)
    settle(0)
    follow(1, 3, 1)
    use_near(1, 0)
    follow(1, 3, 2)
    use_far(1, 0)
    hand_on(1, 3, 0)
    add_lower()
    inverse_next(2)
    use_near(1, 1)
    use_far(1, 1)
    hand_on(1, 3, 1)
    use_near(1, 2)
    hand_on(1, 3, 2)
    use_far(1, 2)
    use_near(1, 3)
    inverse_own[2].wait()
    inverse_wait(2)
    use_far(1, 3)

    for n in (0, 1):
        last(n)
    settle(1)
    left(2, inv.at[2, :, pl.ds(0, 240)])


def on_device(noise_draws, inverse_diagonal, coupling_blocks, ancestor_pick, coupling_lists, live_counts):
    cols = noise_draws.shape[3]
    pair = pltpu.VMEM((2, cols, W), BF16)
    whole, fine = (pltpu.VMEM((2, width, W), BF16) for width in (cols // 2, cols // 4))
    lines = [[[whole] * 2] * (ZS - 2) + [[whole, fine, fine]]] * 2
    dma = pltpu.SemaphoreType.DMA
    scratch = [
        pltpu.VMEM(noise_draws.shape, BF16),
        pltpu.VMEM((3, 2, cols, W), BF16),
        pltpu.VMEM((LEVELS, 2, W, W), BF16),
        pltpu.VMEM((DRAWS, 2, W, W), BF16),
        pltpu.VMEM((DRAWS, 2, W, W), BF16),
        pltpu.VMEM((2, 2, W, W), BF16),
        pair,
        pair,
        lines,
        lines,
        pltpu.VMEM((16, cols, W), BF16),
        pltpu.VMEM((16, cols, W), BF16),
        pltpu.VMEM((ZS, 3, cols, W), BF16),
        pltpu.VMEM((ZS, 3, cols, W), BF16),
        pltpu.VMEM((2, ZS, cols // 2, W), BF16),
        pltpu.VMEM((2, ZS, cols // 2, W), BF16),
        pltpu.VMEM((2, cols, W), F32),
        pltpu.SMEM((2, 2, OWNERS), jnp.int32),
        dma((6,)),
        dma((LEVELS + 6,)),
        dma((LEVELS, 2)),
        dma((2, 4)),
        dma((2, 2, 2)),
        dma((2, 2, 2)),
        dma((2,)),
        dma((2, 2, 3, 3)),
        dma((2, ZS, 3)),
        dma((2, 3, ZS)),
    ]
    smem = pl.BlockSpec(memory_space=pltpu.SMEM)
    anywhere = pl.BlockSpec(memory_space=pl.ANY)
    return pl.pallas_call(
        kernel,
        out_shape=pltpu.VMEM(noise_draws.shape, BF16),
        in_specs=[smem, smem, smem, anywhere, anywhere, anywhere],
        out_specs=pl.BlockSpec(memory_space=pltpu.VMEM),
        scratch_shapes=scratch,
        compiler_params=pltpu.CompilerParams(
            collective_id=0, has_side_effects=True, vmem_limit_bytes=60 * 1024 * 1024
        ),
    )(ancestor_pick, coupling_lists, live_counts, noise_draws, inverse_diagonal, coupling_blocks)


def solution(mesh):
    placed = (
        P(None, "leaf", None, "draw"),
        P(None, "leaf", "draw", None),
        P(None, "leaf", "draw", None, None),
        P(),
        P(None, "leaf", None),
        P(None, "leaf"),
    )
    return jax.shard_map(
        on_device,
        mesh=mesh,
        in_specs=placed,
        out_specs=P(None, "leaf", None, "draw"),
        check_vma=False,
    )
```

```python
import jax
import jax.numpy as jnp
from jax import lax
from jax.experimental import pallas as pl
from jax.experimental.pallas import tpu as pltpu
from jax.sharding import PartitionSpec as P

MESH = pl.DeviceIdType.MESH
YS, ZS, XS, CORES = 4, 4, 4, 2
RING = 2 * ZS
DRAWS = 2 * XS * CORES
LEVELS, OWNERS, SLOTS, W = 3, 16, 16, 256
F32, BF16 = jnp.float32, jnp.bfloat16


def kernel(pick, lists, counts, noise, inverse, blocks, out_v, *scratch):
    (noise_v, flipped, inv, b1, b2, zrel, own0, own1, below, above, t0, t1, sb0, sb1, ry0, ry1, acc, place) = scratch[:18]
    (loc, sent, inv_r, zr, xr, xfr, cr, lr, yr, yrel) = scratch[18:]
    cols = own0.shape[1]
    half = cols // 2
    bf, own, table, send, relay = (b1, b2), (own0, own1), (t0, t1), (sb0, sb1), (ry0, ry1)

    leaf, draw = lax.axis_index("leaf"), lax.axis_index("draw")
    y, zl = lax.div(leaf, ZS), lax.rem(leaf, ZS)
    zh, q = lax.div(draw, XS * CORES), lax.rem(draw, XS * CORES)
    x, c = lax.div(q, CORES), lax.rem(q, CORES)
    z = zh * ZS + zl

    def at(y_, z_, x_, c_):
        return (y_ * ZS + lax.rem(z_, ZS), lax.div(z_, ZS) * (XS * CORES) + x_ * CORES + c_)

    def up(v, step, size):
        return lax.rem(v + step + size, size)

    north, south = at(up(y, 1, YS), z, x, c), at(up(y, -1, YS), z, x, c)
    z_up, z_down = at(y, up(z, 1, RING), x, c), at(y, up(z, -1, RING), x, c)
    z_up2, z_down2 = at(y, up(z, 2, RING), x, c), at(y, up(z, -2, RING), x, c)
    partner = at(y, up(z, ZS, RING), x, c)
    east, west = at(y, z, up(x, 1, XS), c), at(y, z, up(x, -1, XS), c)
    other = at(y, z, x, 1 - c)

    def slot(zh_, x_, c_):
        return zh_ * (XS * CORES) + x_ * CORES + c_

    inside = jnp.logical_and(zl > 0, zl < ZS - 1)
    outside = jnp.logical_not(inside)
    def move(src, dst, s_sem, r_sem, device):
        return pltpu.make_async_remote_copy(
            src_ref=src, dst_ref=dst, send_sem=s_sem, recv_sem=r_sem, device_id=device, device_id_type=MESH
        )

    def put(*args, cond=None):
        run([args], cond)

    def got(dst, r_sem):
        move(dst, dst, r_sem, r_sem, east).wait_recv()

    def left(group, region):
        move(region, region, sent.at[group], sent.at[group], east).wait_send()

    def run(plan, cond=None):
        def body():
            for step in plan:
                if len(step) == 2:
                    got(*step)
                else:
                    move(*step).start()

        if cond is None:
            body()
        else:
            pl.when(cond)(body)

    barrier = pltpu.get_barrier_semaphore()
    peers = [(leaf, zh * (XS * CORES) + lax.rem(q + j, XS * CORES)) for j in (4, 3, 5, 2, 6, 1, 7)]
    greeted = peers + [partner, z_up, z_down, z_up2, z_down2, north, south]
    noise_in = pltpu.make_async_copy(noise, noise_v, loc.at[0])
    noise_in.start()
    for device in greeted:
        pl.semaphore_signal(barrier, inc=1, device_id=device, device_id_type=MESH)
    pl.semaphore_wait(barrier, len(greeted))

    inv_dst = [
        lambda k, level=level: inv.at[level, :, pl.ds(pl.multiple_of(16 * k, 16), 16), :] for level in range(LEVELS)
    ]
    inv_src = [inverse.at[level] for level in range(LEVELS)]
    far = lax.rem(draw + XS * CORES, DRAWS)

    def inverse_across(g):
        put(inv_src[g], inv_dst[g](draw), sent.at[g], inv_r.at[g, 0], partner)

    def inverse_first(g):
        for device in peers:
            put(inv_src[g], inv_dst[g](draw), sent.at[g], inv_r.at[g, 1], device)

    def inverse_next(g):
        got(inv_dst[g](far), inv_r.at[g, 0])
        for device in peers:
            put(inv_dst[g](far), inv_dst[g](far), sent.at[g], inv_r.at[g, 1], device)

    def inverse_wait(g):
        got(inv.at[g, :, pl.ds(0, 224)], inv_r.at[g, 1])

    inverse_own = [pltpu.make_async_copy(inv_src[g], inv_dst[g](draw), loc.at[1 + g]) for g in range(LEVELS)]
    blocks_own = [pltpu.make_async_copy(blocks.at[l, :, 0], bf[l].at[draw], loc.at[4 + l]) for l in (0, 1)]

    def halves(ref):
        return [ref.at[pl.ds(p * (W // 2), W // 2)] for p in (0, 1)]

    ways = ((0, z_up2, -2), (1, z_down2, 2))

    def blocks_z(l, cond=None):
        plan = []
        for p in (0, 1):
            for n, device, _ in ways:
                src, dst = halves(blocks.at[l, n, 0])[p], halves(zrel.at[l, n])[p]
                plan.append((src, dst, sent.at[LEVELS + l], zr.at[l, 0, n, p], device))
        run(plan, cond)

    def blocks_relay(l, cond=None):
        plan = []
        for p in (0, 1):
            for n, device, back in ways:
                k = slot(lax.div(up(z, back, RING), ZS), x, c)
                held, dst = halves(zrel.at[l, n])[p], halves(bf[l].at[k, n])[p]
                plan.append((held, zr.at[l, 0, n, p]))
                plan.append((held, dst, sent.at[LEVELS + l], zr.at[l, 1, n, p], device))
        run(plan, cond)

    def blocks_out(l, u):
        k = (draw, far)[u]
        src = blocks.at[l, :, 0] if u == 0 else bf[l].at[k]
        put(src, bf[l].at[k], sent.at[LEVELS + l], xr.at[l, u, 0], east)
        put(src, bf[l].at[k], sent.at[LEVELS + l], xr.at[l, u, 1], west)
        put(src, bf[l].at[k], sent.at[LEVELS + l], cr.at[l], other)

    def blocks_far(l):
        for n in (0, 1):
            for p in (0, 1):
                got(halves(bf[l].at[far, n])[p], zr.at[l, 1, n, p])
        blocks_out(l, 1)

    def blocks_x(l, u):
        zz = zh if u == 0 else 1 - zh
        k_w, k_e = slot(zz, up(x, -1, XS), c), slot(zz, up(x, 1, XS), c)
        got(bf[l].at[k_w], xr.at[l, u, 0])
        put(bf[l].at[k_w, 0], bf[l].at[k_w, 0], sent.at[LEVELS + l], xfr.at[l, u, 0], east)
        put(bf[l].at[k_w], bf[l].at[k_w], sent.at[LEVELS + l], cr.at[l], other)
        got(bf[l].at[k_e], xr.at[l, u, 1])
        put(bf[l].at[k_e, 1], bf[l].at[k_e, 1], sent.at[LEVELS + l], xfr.at[l, u, 1], west)
        put(bf[l].at[k_e], bf[l].at[k_e], sent.at[LEVELS + l], cr.at[l], other)

    def blocks_x2(l, u):
        k = slot(zh if u == 0 else 1 - zh, up(x, 2, XS), c)
        for n in (0, 1):
            got(bf[l].at[k, n], xfr.at[l, u, n])
            put(bf[l].at[k, n], bf[l].at[k, n], sent.at[LEVELS + l], cr.at[l], other)

    def blocks_wait(l):
        got(bf[l].at[pl.ds(0, DRAWS // 2)], cr.at[l])
        blocks_own[l].wait()

    def parts(r):
        whole = [(0, half, 0), (half, half, 1)]
        return whole if r < ZS - 1 else whole[:1] + [(half, half // 2, 1), (half + half // 2, half // 2, 1)]

    def rows(part):
        return pl.ds(part[0], part[1])

    def relay_rows(part):
        return pl.ds(part[0] % half, part[1])

    def choose(a, s, part, pair):
        src = y * ZS + s

        def wanted(step):
            return pair(pick[a, up(y, step, YS) * ZS + zl, src])

        send[a][s, 0, rows(part)] = wanted(2)
        send[a][s, 1, rows(part)] = wanted(1)
        send[a][s, 2, rows(part)] = wanted(-1)
        table[a][src, rows(part)] = wanted(0)

    def send_far(a, s, i, part):
        way = part[2]
        return [(
            send[a].at[s, 0, rows(part)], relay[a].at[way, s, relay_rows(part)], sent.at[LEVELS + 2 + a],
            yrel.at[a, i, s], (north, south)[way],
        )]

    def send_near(a, s, part):
        dst = table[a].at[y * ZS + s, rows(part)]
        return [
            (send[a].at[s, 1, rows(part)], dst, sent.at[LEVELS + 2 + a], yr.at[a, s, 0], north),
            (send[a].at[s, 2, rows(part)], dst, sent.at[LEVELS + 2 + a], yr.at[a, s, 1], south),
        ]

    def pass_y(a, s, i, part):
        way = part[2]
        src = up(y, (-1, 1)[way], YS) * ZS + s
        held = relay[a].at[way, s, relay_rows(part)]
        return [
            (held, yrel.at[a, i, s]),
            (held, table[a].at[src, rows(part)], sent.at[LEVELS + 2 + a], yr.at[a, s, 2], (north, south)[way]),
        ]

    def first(a, h):
        part = parts(0)[h]
        choose(a, zl, part, lambda n: own[a][n, rows(part)])
        put(own[a].at[:, rows(part)], below[a][0][h], sent.at[LEVELS + 4 + a], lr.at[a, 0, 0, h], z_up, cond=zl < ZS - 1)
        put(own[a].at[:, rows(part)], above[a][0][h], sent.at[LEVELS + 4 + a], lr.at[a, 1, 0, h], z_down, cond=zl > 0)
        run(send_far(a, zl, h, part) + send_near(a, zl, part))

    def follow(a, r, i):
        part = parts(r)[i]
        lines = (
            (below, 0, z_up, zl >= r, zl < ZS - 1, zl - r),
            (above, 1, z_down, zl <= ZS - 1 - r, zl > 0, zl + r),
        )
        for line, way, device, here, more, s in lines:
            held = line[a][r - 1][i]
            run([(held, lr.at[a, way, r - 1, i])], here)
            if r < ZS - 1:
                sends = []
                for j, (start, width, _) in enumerate(parts(r + 1)):
                    if part[0] <= start < part[0] + part[1]:
                        piece = held.at[:, pl.ds(start - part[0], width)]
                        sends.append((piece, line[a][r][j], sent.at[LEVELS + 4 + a], lr.at[a, way, r, j], device))
                run(sends, jnp.logical_and(here, more))
        for line, way, device, here, more, s in lines:
            pl.when(here)(lambda line=line, s=s: choose(a, s, part, lambda n: line[a][r - 1][i][n]))
            run(send_far(a, s, i, part), here)
        ready = {(ZS - 1, 1): [], (ZS - 1, 2): parts(r)[1:]}.get((r, i), [part])
        for line, way, device, here, more, s in lines:
            run([step for each in ready for step in send_near(a, s, each)], here)

    def both(cond, only):
        return cond if only is None else only if cond is None else jnp.logical_and(cond, only)

    def by_round(r, body, only):
        if r == 0:
            body(zl, only)
        else:
            body(zl - r, both(zl >= r, only))
            body(zl + r, both(zl <= ZS - 1 - r, only))

    def hand_on(a, r, i, only=None):
        by_round(r, lambda s, cond: run(pass_y(a, s, i, parts(r)[i]), cond), only)

    def add_source(a, src):
        if a == 0:
            for n in (0, 1):
                k = place[0, n, src]
                alive = (k < counts[0, n]).astype(F32)
                acc[n] += alive * jnp.dot(t0[src], b1[k, n], preferred_element_type=F32)
        else:
            k = place[1, 0, src]
            second = place[1, 1, src]
            term = jnp.dot(t1[src], b2[k, second], preferred_element_type=F32)
            share = second.astype(F32)
            acc[0] += (1.0 - share) * term
            acc[1] += share * term

    def guarded(cond, body):
        if cond is None:
            body()
        else:
            pl.when(cond)(body)

    def use_near(a, r, only=None):
        def body(s, cond):
            def inner():
                add_source(a, y * ZS + s)
                for way, step in ((0, -1), (1, 1)):
                    src = up(y, step, YS) * ZS + s
                    got(table[a].at[src], yr.at[a, s, way])
                    add_source(a, src)

            guarded(cond, inner)

        by_round(r, body, only)

    def use_far(a, r, only=None):
        def body(s, cond):
            def inner():
                src = up(y, 2, YS) * ZS + s
                got(table[a].at[src], yr.at[a, s, 2])
                add_source(a, src)

            guarded(cond, inner)

        by_round(r, body, only)

    def find_places():
        @pl.loop(0, OWNERS)
        def _(o):
            zero = jnp.int32(0)
            for n in (0, 1):
                found = zero
                for k in range(SLOTS):
                    found = jnp.where(lists[0, n, k] == o, k, found)
                place[0, n, o] = found
            k0, n0 = zero, zero
            for k in range(SLOTS // 2):
                first_has, second_has = (lists[1, n, k] == OWNERS + o for n in (0, 1))
                k0 = jnp.where(jnp.logical_or(first_has, second_has), k, k0)
                n0 = jnp.where(second_has, 1, n0)
            place[1, 0, o], place[1, 1, o] = k0, n0

    def add_lower():
        @pl.loop(SLOTS // 2, SLOTS)
        def _(k):
            for n in (0, 1):
                alive = (k < counts[1, n]).astype(F32)
                values = t0[lax.rem(lists[1, n, k], OWNERS)]
                acc[n] += alive * jnp.dot(values, b2[k, n], preferred_element_type=F32)

    def solve(level, n, part):
        right_side = flipped[level, n, rows(part)]
        if level > 0:
            right_side = (right_side.astype(F32) - acc[n, rows(part)]).astype(BF16)
        return jnp.dot(right_side, inv[level, n], preferred_element_type=F32).astype(BF16)

    def clear():
        for n in (0, 1):
            acc[n] = jnp.zeros_like(acc[n])

    def flip(level):
        for n in (0, 1):
            flipped[level, n] = noise_v[level, n].T

    def show(level, ref):
        for n in (0, 1):
            out_v[level, n] = ref[n].T

    def last(n):
        out_v[2, n] = solve(2, n, (0, cols)).T

    def settle(a):
        left(a, inv.at[a, :, pl.ds(0, 240)])
        left(LEVELS + a, table[a])
        left(LEVELS + 2 + a, table[a])
        pl.when(inside)(lambda: left(LEVELS + 4 + a, table[a].at[pl.ds(0, 10)]))
        pl.when(outside)(lambda: left(LEVELS + 4 + a, table[a].at[pl.ds(0, 2)]))

    for copy in inverse_own + blocks_own:
        copy.start()
    inverse_across(0)
    inverse_first(0)
    blocks_z(0)
    inverse_across(1)
    noise_in.wait()
    flip(0)
    inverse_next(0)
    blocks_relay(0)
    inverse_own[0].wait()
    inverse_wait(0)
    for h in (0, 1):
        for n in (0, 1):
            own0[n, rows(parts(0)[h])] = solve(0, n, parts(0)[h])
        first(0, h)
    blocks_out(0, 0)
    find_places()
    inverse_first(1)
    hand_on(0, 0, 0)
    hand_on(0, 0, 1)
    follow(0, 1, 0)
    blocks_x(0, 0)
    blocks_far(0)
    follow(0, 1, 1)
    hand_on(0, 1, 0, outside)
    clear()
    flip(1)
    blocks_x2(0, 0)
    follow(0, 2, 0)
    hand_on(0, 1, 0, inside)
    blocks_x(0, 1)
    hand_on(0, 1, 1, outside)
    inverse_next(1)
    follow(0, 2, 1)
    hand_on(0, 1, 1, inside)
    blocks_x2(0, 1)
    blocks_out(1, 0)
    blocks_z(1, outside)
    hand_on(0, 2, 0, outside)
    blocks_wait(0)
    use_near(0, 0, outside)
    hand_on(0, 2, 0, inside)
    follow(0, 3, 0)
    hand_on(0, 2, 1)
    use_near(0, 0, inside)
    use_far(0, 0)
    follow(0, 3, 1)
    use_near(0, 1)
    follow(0, 3, 2)
    blocks_z(1, inside)
    inverse_across(2)
    hand_on(0, 3, 0)
    blocks_x(1, 0)
    use_far(0, 1)
    blocks_relay(1, inside)
    hand_on(0, 3, 1)
    use_near(0, 2)
    hand_on(0, 3, 2)
    use_far(0, 2)
    inverse_own[1].wait()
    inverse_wait(1)
    blocks_x2(1, 0)
    use_near(0, 3)
    use_far(0, 3)

    for h in (0, 1):
        for n in (0, 1):
            own1[n, rows(parts(0)[h])] = solve(1, n, parts(0)[h])
        first(1, h)
    blocks_relay(1, outside)
    clear()
    show(0, own0)
    flip(2)
    hand_on(1, 0, 0)
    hand_on(1, 0, 1)
    follow(1, 1, 0)
    show(1, own1)
    follow(1, 1, 1)
    hand_on(1, 1, 0, outside)
    follow(1, 2, 0)
    hand_on(1, 1, 0, inside)
    hand_on(1, 1, 1, outside)
    blocks_far(1)
    inverse_first(2)
    follow(1, 2, 1)
    hand_on(1, 1, 1, inside)
    blocks_x(1, 1)
    hand_on(1, 2, 0)
    follow(1, 3, 0)
    hand_on(1, 2, 1)
    blocks_x2(1, 1)
    blocks_wait(1)
    settle(0)
    follow(1, 3, 1)
    use_near(1, 0)
    follow(1, 3, 2)
    use_far(1, 0)
    hand_on(1, 3, 0)
    add_lower()
    inverse_next(2)
    use_near(1, 1)
    use_far(1, 1)
    hand_on(1, 3, 1)
    use_near(1, 2)
    hand_on(1, 3, 2)
    use_far(1, 2)
    use_near(1, 3)
    inverse_own[2].wait()
    inverse_wait(2)
    use_far(1, 3)

    for n in (0, 1):
        last(n)
    settle(1)
    left(2, inv.at[2, :, pl.ds(0, 240)])


def on_device(noise_draws, inverse_diagonal, coupling_blocks, ancestor_pick, coupling_lists, live_counts):
    cols = noise_draws.shape[3]
    pair = pltpu.VMEM((2, cols, W), BF16)
    whole, fine = (pltpu.VMEM((2, width, W), BF16) for width in (cols // 2, cols // 4))
    lines = [[[whole] * 2] * (ZS - 2) + [[whole, fine, fine]]] * 2
    dma = pltpu.SemaphoreType.DMA
    scratch = [
        pltpu.VMEM(noise_draws.shape, BF16),
        pltpu.VMEM((3, 2, cols, W), BF16),
        pltpu.VMEM((LEVELS, 2, W, W), BF16),
        pltpu.VMEM((DRAWS, 2, W, W), BF16),
        pltpu.VMEM((DRAWS, 2, W, W), BF16),
        pltpu.VMEM((2, 2, W, W), BF16),
        pair,
        pair,
        lines,
        lines,
        pltpu.VMEM((16, cols, W), BF16),
        pltpu.VMEM((16, cols, W), BF16),
        pltpu.VMEM((ZS, 3, cols, W), BF16),
        pltpu.VMEM((ZS, 3, cols, W), BF16),
        pltpu.VMEM((2, ZS, cols // 2, W), BF16),
        pltpu.VMEM((2, ZS, cols // 2, W), BF16),
        pltpu.VMEM((2, cols, W), F32),
        pltpu.SMEM((2, 2, OWNERS), jnp.int32),
        dma((6,)),
        dma((LEVELS + 6,)),
        dma((LEVELS, 2)),
        dma((2, 2, 2, 2)),
        dma((2, 2, 2)),
        dma((2, 2, 2)),
        dma((2,)),
        dma((2, 2, 3, 3)),
        dma((2, ZS, 3)),
        dma((2, 3, ZS)),
    ]
    smem = pl.BlockSpec(memory_space=pltpu.SMEM)
    anywhere = pl.BlockSpec(memory_space=pl.ANY)
    return pl.pallas_call(
        kernel,
        out_shape=pltpu.VMEM(noise_draws.shape, BF16),
        in_specs=[smem, smem, smem, anywhere, anywhere, anywhere],
        out_specs=pl.BlockSpec(memory_space=pltpu.VMEM),
        scratch_shapes=scratch,
        compiler_params=pltpu.CompilerParams(
            collective_id=0, has_side_effects=True, vmem_limit_bytes=60 * 1024 * 1024
        ),
    )(ancestor_pick, coupling_lists, live_counts, noise_draws, inverse_diagonal, coupling_blocks)


def solution(mesh):
    placed = (
        P(None, "leaf", None, "draw"),
        P(None, "leaf", "draw", None),
        P(None, "leaf", "draw", None, None),
        P(),
        P(None, "leaf", None),
        P(None, "leaf"),
    )
    return jax.shard_map(
        on_device,
        mesh=mesh,
        in_specs=placed,
        out_specs=P(None, "leaf", None, "draw"),
        check_vma=False,
    )
```
